256 devices in a mesh: col: 16 (over y, z_lo, core), row: 16 (over x, z_hi).
Axes of the slice: x: 4, y: 4, z: 8 (z_hi: 4, z_lo: 2; z = z_hi * 2 + z_lo), core: 2. Of those that a mesh axis runs over, the one named last changes fastest.
Arguments:
- object_field: float32 [2, 4608, 4608], P(None, 'row', 'col'), may hold values from -6 to 6
- probe: float32 [2, 256, 256], replicated, may hold values from -5 to 5
- amplitudes: bfloat16 [16, 16, 8, 256, 256], P('row', 'col'), may hold values from 0 to 2
- offsets: int32 [16, 16, 8, 2], P('row', 'col'), may hold values from 0 to 128
- counts: int32 [16, 16], P('row', 'col'), may hold values from 1 to 8
Outputs:
- updated_object: float32 [2, 4608, 4608], P(None, 'row', 'col')
The draws below stay inside these ranges and needn't reach their ends.
All inputs are finite; a program needn't handle non-finite values.
Results may differ from the reference program's by a relative error of at most 0.0027.
Values sent between devices are 32-bit elements; how exact they have to be, the bound alone decides.
A program may use at most 64 MiB of HBM per device.

```python
import math
import jax
import jax.numpy as jnp
from jax import lax

PROBE = 256
CORE = 288
MARGIN = 48
MAXPOS = 8
PASSES = 2
TILE = 384
NR = 4608
NC = 4608
N_COL = 16
N_ROW = 16


def touch_ends(entries, key, smallest, high):
    place = [jax.random.randint(jax.random.fold_in(key, axis), (), 0, length) for axis, length in enumerate(entries.shape)]
    widest = entries.shape.index(max(entries.shape))
    neighbour = place[:widest] + [(place[widest] + 1) % entries.shape[widest]] + place[widest + 1:]
    return entries.at[tuple(place)].set(smallest).at[tuple(neighbour)].set(high)


def block_levels(rng, shape, cuts, low, largest):
    def one(axis_at, blocks):
        draws = jax.random.uniform(jax.random.fold_in(jax.random.fold_in(rng, 6), axis_at), (blocks,), jnp.float32, low / len(cuts), largest / len(cuts))
        return jnp.repeat(jnp.exp(draws), shape[axis_at] // blocks).reshape((-1,) + (1,) * (len(shape) - axis_at - 1))

    loudness = one(*cuts[0])
    for cut in cuts[1:]:
        loudness = loudness * one(*cut)
    return loudness


def centred(stream_key, dims, width, limit, split=(), held_as=jnp.bfloat16):
    array = width * jax.random.normal(stream_key, dims, jnp.float32)
    if split:
        array = array * block_levels(stream_key, dims, split, -0.22, 0.18)
    return jnp.clip(array, -limit, limit).astype(held_as)


def setup_inputs(seed: int = 0) -> dict:
    arg_keys = jax.random.split(jax.random.key(seed), 6)
    return {
        "object_field": centred(arg_keys[0], (2, NR, NC), 1.0, 6.0, ((1, 16), (2, 16)), jnp.float32),
        "probe": centred(arg_keys[1], (2, PROBE, PROBE), 0.7, 5.0, (), jnp.float32),
        "amplitudes": jnp.clip(2.0 * jax.random.uniform(arg_keys[2], (N_ROW, N_COL, MAXPOS, PROBE, PROBE), jnp.float32) ** block_levels(arg_keys[2], (N_ROW, N_COL, MAXPOS, PROBE, PROBE), ((0, 16), (1, 16)), -0.2, 0.2), 0.0, 2.0).astype(jnp.bfloat16),
        "offsets": touch_ends(jax.random.randint(arg_keys[3], (N_ROW, N_COL, MAXPOS, 2), 0, CORE + 2 * MARGIN - PROBE + 1), jax.random.fold_in(arg_keys[3], 1), 0, CORE + 2 * MARGIN - PROBE).astype(jnp.int32),
        "counts": touch_ends(jax.random.randint(arg_keys[4], (N_ROW, N_COL), 1, MAXPOS + 1), jax.random.fold_in(arg_keys[4], 1), 1, MAXPOS).astype(jnp.int32),
    }


step_size = 0.1
soft_floor = 0.01

def dft_table(direction, length):
    position = jnp.arange(length, dtype=jnp.int32)
    angles = (position[:, None] * position[None, :] % length).astype(jnp.float32) * (2.0 * math.pi / length)
    norm_scale = 1.0 / math.sqrt(length)
    real_part = jnp.cos(angles) * norm_scale
    imag_part = jnp.sin(angles) * (direction * norm_scale)
    return jnp.stack([jnp.stack([real_part, -imag_part]), jnp.stack([imag_part, real_part])]).astype(jnp.bfloat16)

def transform(waves, table):
    table_wide = table.astype(jnp.float32)
    first = jnp.einsum('cdkn,pdnm->pckm', table_wide, waves.astype(jnp.float32), precision=lax.Precision.HIGHEST)
    first = first.astype(jnp.bfloat16).astype(jnp.float32)
    return jnp.einsum('cdkn,pdmn->pcmk', table_wide, first, precision=lax.Precision.HIGHEST)

def position_terms(tile_field, probe, measured, offset_list, live_slots):
    side = probe.shape[-1]
    forward = dft_table(-1.0, side)
    inverse = dft_table(1.0, side)

    def cut_patch(offset):
        return lax.dynamic_slice(tile_field, (jnp.int32(0), offset[0], offset[1]), (2, side, side))
    patches = jax.vmap(cut_patch)(offset_list)
    probe_real, probe_imag = (probe[0], probe[1])
    exit_wave = jnp.stack([probe_real * patches[:, 0] - probe_imag * patches[:, 1], probe_real * patches[:, 1] + probe_imag * patches[:, 0]], axis=1).astype(jnp.bfloat16)
    far_field = transform(exit_wave, forward)
    magnitude = jnp.sqrt(far_field[:, 0] * far_field[:, 0] + far_field[:, 1] * far_field[:, 1] + soft_floor)
    factor = (measured.astype(jnp.float32) / magnitude - 1.0) * live_slots[:, None, None]
    correction = (far_field * factor[:, None]).astype(jnp.bfloat16)
    back_wave = transform(correction, inverse)
    return jnp.stack([probe_real * back_wave[:, 0] + probe_imag * back_wave[:, 1], probe_real * back_wave[:, 1] - probe_imag * back_wave[:, 0]], axis=1)

def add_patches(gradient, terms, offset_list):
    side = terms.shape[-1]

    def add_one(slot, current):
        offset = offset_list[slot]
        start = (jnp.int32(0), offset[0], offset[1])
        patch = lax.dynamic_slice(current, start, (2, side, side))
        return lax.dynamic_update_slice(current, patch + terms[slot], start)
    return lax.fori_loop(0, terms.shape[0], add_one, gradient)

def reference(object_field, probe, amplitudes, offsets, counts):
    current = object_field
    for sweep in range(PASSES):
        padded = jnp.pad(current, ((0, 0), (MARGIN, MARGIN), (MARGIN, MARGIN)))

        def visit(summed, tile_index):
            tile_row = tile_index // N_COL
            tile_col = tile_index % N_COL
            start = (jnp.int32(0), tile_row * CORE, tile_col * CORE)
            tile_field = lax.dynamic_slice(padded, start, (2, TILE, TILE))
            live_slots = (jnp.arange(MAXPOS, dtype=jnp.int32) < counts[tile_row, tile_col]).astype(jnp.float32)
            terms = position_terms(tile_field, probe, amplitudes[tile_row, tile_col], offsets[tile_row, tile_col], live_slots)
            local_sum = add_patches(jnp.zeros((2, TILE, TILE), jnp.float32), terms, offsets[tile_row, tile_col])
            block = lax.dynamic_slice(summed, start, (2, TILE, TILE))
            return (lax.dynamic_update_slice(summed, block + local_sum, start), None)
        summed, unused = lax.scan(visit, jnp.zeros(padded.shape, jnp.float32), jnp.arange(N_ROW * N_COL, dtype=jnp.int32))
        current = current + step_size * summed[:, MARGIN:-MARGIN, MARGIN:-MARGIN]
    return current
```

```python
import functools
import math

import jax
import jax.numpy as jnp
import numpy as np
from jax import lax
from jax.experimental import pallas as pl
from jax.experimental.pallas import tpu as pltpu
from jax.sharding import PartitionSpec as P

MARGIN = 48
PASSES = 2
SIDE = 256
HALF = 128
CORE = 288
TILE = 384
SLOTS = 8
STEP = 0.1
FLOOR = 0.01
F32 = jnp.float32
BF16 = jnp.bfloat16

EDGE = ((0, 48), (80, 48))
INNER = ((48, 32), (128, 128))
N_EDGE = 96
N_INNER = 160


def half_tables():
    position = np.arange(SIDE)
    angle = (position[:, None] * position[None, :] % SIDE) * (2.0 * math.pi / SIDE)
    scale = 1.0 / math.sqrt(SIDE)
    cosine, sine = np.cos(angle) * scale, np.sin(angle) * scale
    table = np.concatenate([cosine[:HALF], cosine[HALF : HALF + 1], sine[1:HALF]])
    order = np.concatenate([np.arange(HALF), [HALF], np.arange(SIDE - 1, HALF, -1)])
    swap = np.zeros((SIDE, SIDE), np.float32)
    swap[np.arange(SIDE), order] = 1.0
    return [a.astype(jnp.bfloat16) for a in (table, table.T, swap)]


def mm(a, b):
    return jnp.dot(a, b, preferred_element_type=F32)


def lane_iota(rows):
    return lax.broadcasted_iota(jnp.int32, (rows, HALF), 1)


def row_iota(rows, start):
    return lax.broadcasted_iota(jnp.int32, (rows, HALF), 0) + start


def blk(n):
    return pl.ds(n * HALF, HALF)


def chunks(ranges, step):
    for start, length in ranges:
        for at in range(start, start + length, step):
            yield at


def kernel(
    off, cnt, obj, probe, amp, table, table_t, swap, out,
    ob, pb, ab, tv, ttv, sv,
    pr, ap, hb, wb, qb, xe, xi, cur, g,
    row_in, col_s, col_in, grow_s, grow_in, gcol_s, gcol_in, frow_s, frow_in, fcol_s, fcol_in,
    load_sem, send_sem, recv_sem,
):
    n_row, n_col = lax.axis_size("row"), lax.axis_size("col")
    me_r, me_c = lax.axis_index("row"), lax.axis_index("col")
    has = {("row", 0): me_r > 0, ("row", 1): me_r < n_row - 1, ("col", 0): me_c > 0, ("col", 1): me_c < n_col - 1}
    to = {("row", 0): me_r - 1, ("row", 1): me_r + 1, ("col", 0): me_c - 1, ("col", 1): me_c + 1}

    loads = [
        pltpu.make_async_copy(src, dst, load_sem.at[i])
        for i, (src, dst) in enumerate(
            ((obj, ob), (probe, pb), (amp, ab), (table, tv), (table_t, ttv), (swap, sv))
        )
    ]
    for copy in loads:
        copy.start()

    barrier = pltpu.get_barrier_semaphore()
    for key, ok in has.items():
        @pl.when(ok)
        def _(key=key):
            pl.semaphore_signal(barrier, inc=1, device_id={key[0]: to[key]}, device_id_type=pl.DeviceIdType.MESH)
    pl.semaphore_wait(barrier, sum(ok.astype(jnp.int32) for ok in has.values()))

    def remote(axis, side, number, src, dst):
        return pltpu.make_async_remote_copy(
            src_ref=src,
            dst_ref=dst,
            send_sem=send_sem.at[number * 2 + side],
            recv_sem=recv_sem.at[number * 2 + (1 - side)],
            device_id={axis: to[axis, side]},
            device_id_type=pl.DeviceIdType.MESH,
        )

    def send(axis, side, number, src, dst):
        @pl.when(has[axis, side])
        def _():
            remote(axis, side, number, src, dst).start()

    def sent(axis, side, number, src, dst):
        @pl.when(has[axis, side])
        def _():
            remote(axis, side, number, src, dst).wait_send()

    def arrived(axis, side, number, src, dst):
        @pl.when(has[axis, side])
        def _():
            pltpu.make_async_remote_copy(
                src_ref=src, dst_ref=dst,
                send_sem=send_sem.at[number * 2 + 1 - side],
                recv_sem=recv_sem.at[number * 2 + side],
                device_id={axis: to[axis, side]},
                device_id_type=pl.DeviceIdType.MESH,
            ).wait_recv()

    lanes8 = lane_iota(8)

    def halo_row(side):
        start = 0 if side == 0 else CORE - MARGIN
        return ob.at[:, pl.ds(start, MARGIN), :], row_in.at[1 - side]

    loads[0].wait()
    for side in (0, 1):
        send("row", side, 0, *halo_row(side))

    def place(comp, row, values):
        n = values[0].shape[0]
        lane = lane_iota(n)
        rolled = [pltpu.roll(v, MARGIN, 1) for v in values]
        cur[comp, pl.ds(row, n), blk(0)] = jnp.where(lane < MARGIN, 0.0, rolled[0])
        cur[comp, pl.ds(row, n), blk(1)] = jnp.where(lane < MARGIN, rolled[0], rolled[1])
        cur[comp, pl.ds(row, n), blk(2)] = jnp.where(
            lane < MARGIN, rolled[1], jnp.where(lane < 80, rolled[2], 0.0))

    def place_rows(ref, n, first):
        @pl.loop(0, n // 16)
        def _(i):
            at = pl.multiple_of(i * 16, 16)
            for comp in (0, 1):
                values = [ref[comp, pl.ds(at, 16), blk(0)], ref[comp, pl.ds(at, 16), blk(1)],
                          jnp.concatenate([ref[comp, pl.ds(at, 16), pl.ds(256, 32)], jnp.zeros((16, 96), F32)], 1)]
                place(comp, first + at, values)

    place_rows(ob, CORE, MARGIN)

    def halo_col_pack(row, at, n):
        lane = lane_iota(n)
        rows = pl.ds(row, n)
        col_s[0, pl.ds(at, n), :] = jnp.where(
            lane < 64, pltpu.roll(cur[0, rows, blk(0)], HALF - 48, 1), pltpu.roll(cur[1, rows, blk(0)], 16, 1))
        col_s[1, pl.ds(at, n), :] = jnp.where(
            lane < 64, pltpu.roll(cur[0, rows, blk(2)], HALF - 32, 1), pltpu.roll(cur[1, rows, blk(2)], 32, 1))

    def halo_col_unpack(side, row, at, n):
        lane = lane_iota(n)
        rows = pl.ds(row, n)
        strip = col_in[side, pl.ds(at, n), :]
        if side == 0:
            for comp, shift in ((0, 0), (1, 64)):
                new = strip if shift == 0 else pltpu.roll(strip, shift, 1)
                cur[comp, rows, blk(0)] = jnp.where(lane < 48, new, cur[comp, rows, blk(0)])
        else:
            for comp, shift in ((0, 80), (1, 16)):
                cur[comp, rows, blk(2)] = jnp.where(lane >= 80, pltpu.roll(strip, shift, 1), cur[comp, rows, blk(2)])

    def col_part(side, part):
        at, n = ((0, CORE), (CORE, 2 * MARGIN))[part]
        return col_s.at[side, pl.ds(at, n), :], col_in.at[1 - side, pl.ds(at, n), :]

    def col_part_in(side, part):
        at, n = ((0, CORE), (CORE, 2 * MARGIN))[part]
        return col_s.at[1 - side, pl.ds(at, n), :], col_in.at[side, pl.ds(at, n), :]

    @pl.loop(0, CORE // 16)
    def _(i):
        halo_col_pack(MARGIN + pl.multiple_of(i * 16, 16), pl.multiple_of(i * 16, 16), 16)

    for side in (0, 1):
        send("col", side, 1, *col_part(side, 0))

    loads[1].wait()
    loads[2].wait()
    for copy in loads[3:]:
        copy.wait()
    live_count = cnt[0, 0]

    @pl.loop(0, SLOTS)
    def _(s):
        r, c = off[0, 0, s, 0], off[0, 0, s, 1]
        live = jnp.where(s < live_count, 1.0, 0.0).astype(F32)
        for comp in (0, 1):
            pr[s, comp] = pltpu.roll(pltpu.roll(pb[comp], r, 0), c, 1) * live
        ap[s] = mm(mm(sv[...], ab[0, 0, s]).astype(BF16), sv[...]).astype(BF16)

    def cols_fix(plain, other, lane):
        return jnp.where(lane == 0, other, plain)

    def forward_rows(s, ranges, total, xbuf):
        r, c = off[0, 0, s, 0], off[0, 0, s, 1]
        at = 0
        for m in chunks(ranges, 16):
            lane = lane_iota(16)
            hi_c = lane < c
            patch = []
            for comp in (0, 1):
                if m < HALF:
                    hi_r = row_iota(16, m) < r
                    three = [
                        jnp.where(hi_r, cur[comp, pl.ds(m + SIDE, 16), blk(b)], cur[comp, pl.ds(m, 16), blk(b)])
                        for b in range(3)
                    ]
                else:
                    three = [cur[comp, pl.ds(m, 16), blk(b)] for b in range(3)]
                patch.append((jnp.where(hi_c, three[2], three[0]), three[1]))
            for b in (0, 1):
                p0, p1 = pr[s, 0, pl.ds(m, 16), blk(b)], pr[s, 1, pl.ds(m, 16), blk(b)]
                xbuf[pl.ds(at, 16), blk(b)] = (p0 * patch[0][b] - p1 * patch[1][b]).astype(BF16)
                xbuf[pl.ds(total + at, 16), blk(b)] = (p0 * patch[1][b] + p1 * patch[0][b]).astype(BF16)
            at += 16
        v = mm(xbuf[...], ttv[...])
        at = 0
        lane = lane_iota(16)
        for m in chunks(ranges, 16):
            c_r, s_r = v[at : at + 16, :HALF], v[at : at + 16, HALF:]
            c_i, s_i = v[total + at : total + at + 16, :HALF], v[total + at : total + at + 16, HALF:]
            hb[s, pl.ds(m, 16), blk(0)] = cols_fix(c_r + s_i, c_r, lane).astype(BF16)
            hb[s, pl.ds(m, 16), blk(1)] = cols_fix(c_r - s_i, s_r, lane).astype(BF16)
            hb[s, pl.ds(m, 16), blk(2)] = cols_fix(c_i - s_r, c_i, lane).astype(BF16)
            hb[s, pl.ds(m, 16), blk(3)] = cols_fix(c_i + s_r, s_i, lane).astype(BF16)
            at += 16

    q_row = {}
    at = 0
    for m in chunks(EDGE, 16):
        q_row[m] = (at, N_EDGE + at)
        at += 16
    at = 2 * N_EDGE
    for m in chunks(INNER, 16):
        q_row[m] = (at, N_INNER + at)
        at += 16

    def middle(s):
        u = mm(tv[...], hb[s])
        lane = lane_iota(16)
        for k in range(0, HALF, 16):
            for b in (0, 1):
                lo, hi = slice(k, k + 16), slice(HALF + k, HALF + k + 16)
                re, im = slice(b * HALF, b * HALF + HALF), slice(SIDE + b * HALF, SIDE + b * HALF + HALF)
                c_r, s_r, c_i, s_i = u[lo, re], u[hi, re], u[lo, im], u[hi, im]
                p_r, p_i, m_r, m_i = c_r + s_i, c_i - s_r, c_r - s_i, c_i + s_r
                if k == 0:
                    first = row_iota(16, 0) == 0
                    p_r, p_i = jnp.where(first, c_r, p_r), jnp.where(first, c_i, p_i)
                    m_r, m_i = jnp.where(first, s_r, m_r), jnp.where(first, s_i, m_i)
                f_p = ap[s, pl.ds(k, 16), blk(b)].astype(F32) * lax.rsqrt(p_r * p_r + p_i * p_i + FLOOR) - 1.0
                f_m = ap[s, pl.ds(HALF + k, 16), blk(b)].astype(F32) * lax.rsqrt(m_r * m_r + m_i * m_i + FLOOR) - 1.0
                p_r, p_i, m_r, m_i = p_r * f_p, p_i * f_p, m_r * f_m, m_i * f_m
                a_r, a_i, nb_i, b_r = p_r + m_r, p_i + m_i, m_i - p_i, p_r - m_r
                if k == 0:
                    a_r, a_i = jnp.where(first, p_r, a_r), jnp.where(first, p_i, a_i)
                    nb_i, b_r = jnp.where(first, m_r, nb_i), jnp.where(first, m_i, b_r)
                wb[pl.ds(k, 16), blk(b)] = a_r.astype(BF16)
                wb[pl.ds(k, 16), blk(2 + b)] = a_i.astype(BF16)
                wb[pl.ds(HALF + k, 16), blk(b)] = nb_i.astype(BF16)
                wb[pl.ds(HALF + k, 16), blk(2 + b)] = b_r.astype(BF16)
        y = mm(ttv[...], wb[...])
        for m in range(0, SIDE, 16):
            rows = slice(m, m + 16)
            p_r, m_r, p_i, m_i = (y[rows, b * HALF : b * HALF + HALF] for b in range(4))
            re, im = q_row[m]
            qb[s, pl.ds(re, 16), blk(0)] = cols_fix(p_r + m_r, p_r, lane).astype(BF16)
            qb[s, pl.ds(re, 16), blk(1)] = cols_fix(m_i - p_i, m_r, lane).astype(BF16)
            qb[s, pl.ds(im, 16), blk(0)] = cols_fix(p_i + m_i, p_i, lane).astype(BF16)
            qb[s, pl.ds(im, 16), blk(1)] = cols_fix(p_r - m_r, m_i, lane).astype(BF16)

    def backward_rows(s, ranges, total, q_at):
        r, c = off[0, 0, s, 0], off[0, 0, s, 1]
        v = mm(qb[s, pl.ds(q_at, 2 * total), :], tv[...])
        at = 0
        for m in chunks(ranges, 16):
            hi_c = lane_iota(16) < c
            terms = ([], [])
            for b in (0, 1):
                b_r = v[at : at + 16, b * HALF : b * HALF + HALF]
                b_i = v[total + at : total + at + 16, b * HALF : b * HALF + HALF]
                p0, p1 = pr[s, 0, pl.ds(m, 16), blk(b)], pr[s, 1, pl.ds(m, 16), blk(b)]
                terms[0].append(p0 * b_r + p1 * b_i)
                terms[1].append(p0 * b_i - p1 * b_r)
            for comp in (0, 1):
                high = jnp.where(hi_c, terms[comp][0], 0.0)
                three = (terms[comp][0] - high, terms[comp][1], high)
                for b in range(3):
                    if m < HALF:
                        below = jnp.where(row_iota(16, m) < r, three[b], 0.0)
                        g[comp, pl.ds(m, 16), blk(b)] += three[b] - below
                        g[comp, pl.ds(m + SIDE, 16), blk(b)] += below
                    else:
                        g[comp, pl.ds(m, 16), blk(b)] += three[b]
            at += 16

    def zero_gradient():
        @pl.loop(0, TILE // 16)
        def _(i):
            for comp in (0, 1):
                g[comp, pl.ds(pl.multiple_of(i * 16, 16), 16), :] = jnp.zeros((16, TILE), F32)

    def each_slot(f):
        @pl.loop(0, SLOTS)
        def _(s):
            f(s)

    for side in (0, 1):
        arrived("col", side, 1, *col_part_in(side, 0))

        @pl.when(has["col", side])
        def _(side=side):
            @pl.loop(0, CORE // 16)
            def _(i):
                halo_col_unpack(side, MARGIN + pl.multiple_of(i * 16, 16), pl.multiple_of(i * 16, 16), 16)

    zero_gradient()
    each_slot(lambda s: forward_rows(s, INNER, N_INNER, xi))

    for side in (0, 1):
        first = 0 if side == 0 else TILE - MARGIN
        arrived("row", side, 0, ob.at[:, pl.ds(0, MARGIN), :], row_in.at[side])

        @pl.when(has["row", side])
        def _(side=side, first=first):
            place_rows(row_in.at[side], MARGIN, first)

        @pl.when(jnp.logical_not(has["row", side]))
        def _(first=first):
            for comp in (0, 1):
                cur[comp, pl.ds(first, MARGIN), :] = jnp.zeros((MARGIN, TILE), F32)

        for j in range(0, MARGIN, 16):
            halo_col_pack(first + j, CORE + side * MARGIN + j, 16)
    for side in (0, 1):
        send("col", side, 2, *col_part(side, 1))
    for side in (0, 1):
        arrived("col", side, 2, *col_part_in(side, 1))

        @pl.when(has["col", side])
        def _(side=side):
            for part in (0, 1):
                for j in range(0, MARGIN, 16):
                    halo_col_unpack(side, (0, TILE - MARGIN)[part] + j, CORE + part * MARGIN + j, 16)

    each_slot(lambda s: forward_rows(s, EDGE, N_EDGE, xe))
    each_slot(middle)
    each_slot(lambda s: backward_rows(s, EDGE, N_EDGE, 0))

    WIDE = 2 * MARGIN

    def stage(dst, src_row, n_rows):
        for comp in (0, 1):
            for j in range(0, n_rows, 16):
                dst[comp, pl.ds(j, 16), :] = g[comp, pl.ds(src_row + j, 16), :]

    each_slot(lambda s: backward_rows(s, INNER, N_INNER, 2 * N_EDGE))

    for side in (0, 1):
        stage(grow_s.at[side], 0 if side == 0 else TILE - WIDE, WIDE)
    for side in (0, 1):
        send("row", side, 3, grow_s.at[side], grow_in.at[1 - side])

    def gcol_rows(part):
        return ((WIDE, 192),) if part == 0 else ((0, WIDE), (TILE - WIDE, WIDE))

    def gcol_index(part):
        first, second = (WIDE, 2 * WIDE) if part == 0 else (0, TILE - WIDE)
        return [(first + j, second + j, j) for j in range(0, WIDE, 16)]

    def gcol_pack(part):
        lane = lane_iota(16)
        base = part * 288
        for row_a, row_b, j in gcol_index(part):
            for side in (0, 1):
                kept = []
                for row, at in ((row_a, j), (row_b, WIDE + j)):
                    re = g[0, pl.ds(row, 16), blk(0 if side == 0 else 2)]
                    im = g[1, pl.ds(row, 16), blk(0 if side == 0 else 2)]
                    if side == 1:
                        re, im = pltpu.roll(re, 96, 1), pltpu.roll(im, 96, 1)
                    gcol_s[side, pl.ds(base + at, 16), :] = jnp.where(lane < 96, re, pltpu.roll(im, 96, 1))
                    kept.append(im)
                gcol_s[side, pl.ds(base + 192 + j, 16), :] = jnp.where(
                    lane < 64, pltpu.roll(kept[0], 96, 1), pltpu.roll(kept[1], 32, 1))

    def gcol_unpack(side, part):
        lane = lane_iota(16)
        base = part * 288
        b = 0 if side == 0 else 2
        for row_a, row_b, j in gcol_index(part):
            rest = gcol_in[side, pl.ds(base + 192 + j, 16), :]
            for row, at, shift in ((row_a, j, 32), (row_b, WIDE + j, 96)):
                strip = gcol_in[side, pl.ds(base + at, 16), :]
                re = jnp.where(lane < 96, strip, 0.0)
                im = jnp.where(lane < 32, pltpu.roll(strip, 32, 1), pltpu.roll(rest, shift, 1))
                im = jnp.where(lane < 96, im, 0.0)
                if side == 1:
                    re, im = pltpu.roll(re, 32, 1), pltpu.roll(im, 32, 1)
                g[0, pl.ds(row, 16), blk(b)] += re
                g[1, pl.ds(row, 16), blk(b)] += im

    def gcol_part(side, part):
        rows = pl.ds(part * 288, 288)
        return gcol_s.at[side, rows, :], gcol_in.at[1 - side, rows, :]

    def gcol_part_in(side, part):
        rows = pl.ds(part * 288, 288)
        return gcol_s.at[1 - side, rows, :], gcol_in.at[side, rows, :]

    gcol_pack(0)
    for side in (0, 1):
        send("col", side, 4, *gcol_part(side, 0))
    for side in (0, 1):
        arrived("row", side, 3, grow_s.at[1 - side], grow_in.at[side])

        @pl.when(has["row", side])
        def _(side=side):
            first = 0 if side == 0 else TILE - WIDE
            for comp in (0, 1):
                for j in range(0, WIDE, 16):
                    g[comp, pl.ds(first + j, 16), :] += grow_in[side, comp, pl.ds(j, 16), :]
    gcol_pack(1)
    for side in (0, 1):
        send("col", side, 5, *gcol_part(side, 1))
    for part in (0, 1):
        for side in (0, 1):
            arrived("col", side, 4 + part, *gcol_part_in(side, part))

            @pl.when(has["col", side])
            def _(side=side, part=part):
                gcol_unpack(side, part)

    @pl.loop(0, TILE // 16)
    def _(i):
        at = pl.multiple_of(i * 16, 16)
        lane, row = lane_iota(16), row_iota(16, at)
        keep = [None] * 3
        row_ok = jnp.logical_and(jnp.logical_or(row >= MARGIN, has["row", 0]),
                                 jnp.logical_or(row < TILE - MARGIN, has["row", 1]))
        keep[0] = jnp.logical_and(row_ok, jnp.logical_or(lane >= MARGIN, has["col", 0]))
        keep[1] = row_ok
        keep[2] = jnp.logical_and(row_ok, jnp.logical_or(lane < 80, has["col", 1]))
        for comp in (0, 1):
            for b in range(3):
                cur[comp, pl.ds(at, 16), blk(b)] += jnp.where(
                    keep[b], STEP * g[comp, pl.ds(at, 16), blk(b)], 0.0)

    zero_gradient()
    each_slot(lambda s: forward_rows(s, INNER, N_INNER, xi))
    each_slot(lambda s: forward_rows(s, EDGE, N_EDGE, xe))
    each_slot(middle)
    each_slot(lambda s: backward_rows(s, EDGE, N_EDGE, 0))

    for side in (0, 1):
        first = 0 if side == 0 else TILE - MARGIN
        stage(frow_s.at[side], first, MARGIN)
    for side in (0, 1):
        send("row", side, 6, frow_s.at[side], frow_in.at[1 - side])
    each_slot(lambda s: backward_rows(s, INNER, N_INNER, 2 * N_EDGE))

    def fcol_index(part):
        if part == 0:
            return [(2 * MARGIN + j, j) for j in range(0, 192, 16)]
        return [(MARGIN + j, 192 + j) for j in range(0, MARGIN, 16)] + [
            (TILE - 2 * MARGIN + j, 240 + j) for j in range(0, MARGIN, 16)]

    def fcol_pack(part):
        lane = lane_iota(16)
        for row, at in fcol_index(part):
            rows, to_rows = pl.ds(row, 16), pl.ds(at, 16)
            fcol_s[0, to_rows, :] = jnp.where(
                lane < 64, g[0, rows, blk(0)], pltpu.roll(g[1, rows, blk(0)], 64, 1))
            fcol_s[1, to_rows, :] = jnp.where(
                lane < 64, pltpu.roll(g[0, rows, blk(2)], 48, 1), pltpu.roll(g[1, rows, blk(2)], 112, 1))

    def fcol_unpack(side, part):
        lane = lane_iota(16)
        for row, at in fcol_index(part):
            strip = fcol_in[side, pl.ds(at, 16), :]
            if side == 0:
                b, ok = 0, jnp.logical_and(lane >= 48, lane < 96)
                pair = (pltpu.roll(strip, 48, 1), pltpu.roll(strip, 112, 1))
            else:
                b, ok = 2, jnp.logical_and(lane >= 32, lane < 80)
                pair = (pltpu.roll(strip, 32, 1), pltpu.roll(strip, 96, 1))
            for comp in (0, 1):
                g[comp, pl.ds(row, 16), blk(b)] += jnp.where(ok, pair[comp], 0.0)

    def fcol_part(side, part):
        rows = pl.ds(*((0, 192), (192, 96))[part])
        return fcol_s.at[side, rows, :], fcol_in.at[1 - side, rows, :]

    def fcol_part_in(side, part):
        rows = pl.ds(*((0, 192), (192, 96))[part])
        return fcol_s.at[1 - side, rows, :], fcol_in.at[side, rows, :]

    fcol_pack(0)
    for side in (0, 1):
        send("col", side, 7, *fcol_part(side, 0))
    for side in (0, 1):
        arrived("row", side, 6, frow_s.at[1 - side], frow_in.at[side])

        @pl.when(has["row", side])
        def _(side=side):
            first = MARGIN if side == 0 else TILE - 2 * MARGIN
            for comp in (0, 1):
                for j in range(0, MARGIN, 16):
                    g[comp, pl.ds(first + j, 16), :] += frow_in[side, comp, pl.ds(j, 16), :]
    fcol_pack(1)
    for side in (0, 1):
        send("col", side, 8, *fcol_part(side, 1))
    for part in (0, 1):
        for side in (0, 1):
            arrived("col", side, 7 + part, *fcol_part_in(side, part))

            @pl.when(has["col", side])
            def _(side=side, part=part):
                fcol_unpack(side, part)

    @pl.loop(0, CORE // 16)
    def _(i):
        at = pl.multiple_of(i * 16, 16)
        lane = lane_iota(16)
        for comp in (0, 1):
            v = [
                pltpu.roll(cur[comp, pl.ds(MARGIN + at, 16), blk(b)] + STEP * g[comp, pl.ds(MARGIN + at, 16), blk(b)],
                           80, 1)
                for b in range(3)
            ]
            out[comp, pl.ds(at, 16), blk(0)] = jnp.where(lane < 80, v[0], v[1])
            out[comp, pl.ds(at, 16), blk(1)] = jnp.where(lane < 80, v[1], v[2])
            out[comp, pl.ds(at, 16), pl.ds(256, 32)] = v[2][:, :32]

    for side in (0, 1):
        sent("row", side, 0, *halo_row(side))
        sent("col", side, 1, *col_part(side, 0))
        sent("col", side, 2, *col_part(side, 1))
        sent("row", side, 3, grow_s.at[side], grow_in.at[1 - side])
        sent("col", side, 4, *gcol_part(side, 0))
        sent("col", side, 5, *gcol_part(side, 1))
        sent("row", side, 6, frow_s.at[side], frow_in.at[1 - side])
        sent("col", side, 7, *fcol_part(side, 0))
        sent("col", side, 8, *fcol_part(side, 1))


def shards(object_field, probe, amplitudes, offsets, counts):
    table, table_t, swap = (jnp.asarray(a) for a in half_tables())
    anywhere = pl.BlockSpec(memory_space=pl.ANY)
    scalars = pl.BlockSpec(memory_space=pltpu.SMEM)
    v32 = lambda *shape: pltpu.VMEM(shape, F32)
    v16 = lambda *shape: pltpu.VMEM(shape, BF16)
    return pl.pallas_call(
        kernel,
        out_shape=jax.ShapeDtypeStruct(object_field.shape, F32),
        in_specs=[scalars, scalars] + [anywhere] * 6,
        out_specs=pl.BlockSpec(memory_space=pltpu.VMEM),
        scratch_shapes=[
            v32(2, CORE, CORE), v32(2, SIDE, SIDE), v16(1, 1, SLOTS, SIDE, SIDE),
            v16(SIDE, SIDE), v16(SIDE, SIDE), v16(SIDE, SIDE),
            v32(SLOTS, 2, SIDE, SIDE), v16(SLOTS, SIDE, SIDE),
            v16(SLOTS, SIDE, 2 * SIDE), v16(SIDE, 2 * SIDE), v16(SLOTS, 2 * SIDE, SIDE),
            v16(2 * N_EDGE, SIDE), v16(2 * N_INNER, SIDE),
            v32(2, TILE, TILE), v32(2, TILE, TILE),
            v32(2, 2, MARGIN, CORE), v32(2, TILE, HALF), v32(2, TILE, HALF),
            v32(2, 2, 2 * MARGIN, TILE), v32(2, 2, 2 * MARGIN, TILE),
            v32(2, 576, HALF), v32(2, 576, HALF),
            v32(2, 2, MARGIN, TILE), v32(2, 2, MARGIN, TILE),
            v32(2, CORE, HALF), v32(2, CORE, HALF),
            pltpu.SemaphoreType.DMA((6,)),
            pltpu.SemaphoreType.DMA((18,)),
            pltpu.SemaphoreType.DMA((18,)),
        ],
        compiler_params=pltpu.CompilerParams(
            collective_id=0, has_side_effects=True, vmem_limit_bytes=60 * 1024 * 1024),
        name="ptycho",
    )(offsets, counts, object_field, probe, amplitudes, table, table_t, swap)


def solution(mesh):
    return jax.shard_map(
        shards,
        mesh=mesh,
        in_specs=(
            P(None, "row", "col"),
            P(),
            P("row", "col", None, None, None),
            P("row", "col", None, None),
            P("row", "col"),
        ),
        out_specs=P(None, "row", "col"),
        check_vma=False,
    )
```

```python
import functools
import math

import jax
import jax.numpy as jnp
import numpy as np
from jax import lax
from jax.experimental import pallas as pl
from jax.experimental.pallas import tpu as pltpu
from jax.sharding import PartitionSpec as P

MARGIN = 48
PASSES = 2
SIDE = 256
HALF = 128
CORE = 288
TILE = 384
SLOTS = 8
STEP = 0.1
FLOOR = 0.01
F32 = jnp.float32
BF16 = jnp.bfloat16

WIDE = 2 * MARGIN

EDGE, INNER = 0, HALF


def half_tables():
    position = np.arange(SIDE)
    angle = (position[:, None] * position[None, :] % SIDE) * (2.0 * math.pi / SIDE)
    scale = 1.0 / math.sqrt(SIDE)
    cosine, sine = np.cos(angle) * scale, np.sin(angle) * scale
    table = np.concatenate([cosine[:HALF], cosine[HALF : HALF + 1], sine[1:HALF]])
    order = np.concatenate([np.arange(HALF), [HALF], np.arange(SIDE - 1, HALF, -1)])
    swap = np.zeros((SIDE, SIDE), np.float32)
    swap[np.arange(SIDE), order] = 1.0
    return [a.astype(jnp.bfloat16) for a in (table, table.T, swap)]


def mm(a, b):
    return jnp.dot(a, b, preferred_element_type=F32)


def lane_iota(rows):
    return lax.broadcasted_iota(jnp.int32, (rows, HALF), 1)


def row_iota(rows, start):
    return lax.broadcasted_iota(jnp.int32, (rows, HALF), 0) + start


def blk(n):
    return pl.ds(n * HALF, HALF)


def kernel(
    off, cnt, obj, probe, amp, table, table_t, swap, out,
    ob, pb, ab, tv, ttv, sv,
    pr, ap, hb, wb, qb, xb, cur, ga, gb,
    row_in, col_s, col_in, grow_s, grow_in, gcol_s, gcol_in, frow_s, frow_in, fcol_s, fcol_in,
    load_sem, send_sem, recv_sem,
):
    n_row, n_col = lax.axis_size("row"), lax.axis_size("col")
    me_r, me_c = lax.axis_index("row"), lax.axis_index("col")
    has = {("row", 0): me_r > 0, ("row", 1): me_r < n_row - 1, ("col", 0): me_c > 0, ("col", 1): me_c < n_col - 1}
    to = {("row", 0): me_r - 1, ("row", 1): me_r + 1, ("col", 0): me_c - 1, ("col", 1): me_c + 1}
    sides = [(axis, side) for axis in ("row", "col") for side in (0, 1)]
    corners = [(a, b) for a in (0, 1) for b in (0, 1)]

    def peer(key):
        if key in has:
            return has[key], {key[0]: to[key]}
        rows, cols = ("row", key[0]), ("col", key[1])
        return jnp.logical_and(has[rows], has[cols]), {"row": to[rows], "col": to[cols]}

    def other(key):
        return (key[0], 1 - key[1]) if key in has else (1 - key[0], 1 - key[1])

    loads = [
        pltpu.make_async_copy(src, dst, load_sem.at[i])
        for i, (src, dst) in enumerate(
            ((obj, ob), (probe, pb), (amp, ab), (table, tv), (table_t, ttv), (swap, sv))
        )
    ]
    for copy in loads:
        copy.start()

    barrier = pltpu.get_barrier_semaphore()
    for key in sides + corners:
        ok, device = peer(key)

        @pl.when(ok)
        def _(device=device):
            pl.semaphore_signal(barrier, inc=1, device_id=device, device_id_type=pl.DeviceIdType.MESH)
    pl.semaphore_wait(barrier, sum(peer(key)[0].astype(jnp.int32) for key in sides + corners))

    kinds, started = {}, []

    def semaphore(kind, key):
        return kinds.setdefault((kind, key), len(kinds))

    def remote(key, kind, src, dst, outgoing):
        here, there = (key, other(key)) if outgoing else (other(key), key)
        return pltpu.make_async_remote_copy(
            src_ref=src, dst_ref=dst,
            send_sem=send_sem.at[semaphore(kind, here)],
            recv_sem=recv_sem.at[semaphore(kind, there)],
            device_id=peer(key)[1],
            device_id_type=pl.DeviceIdType.MESH,
        )

    def send(key, kind, src, dst):
        started.append((key, kind, src, dst))

        @pl.when(peer(key)[0])
        def _():
            remote(key, kind, src, dst, True).start()

    def arrived(key, kind, src, dst):
        @pl.when(peer(key)[0])
        def _():
            remote(key, kind, src, dst, False).wait_recv()

    loads[0].wait()
    for side in (0, 1):
        start = 0 if side == 0 else CORE - MARGIN
        send(("row", side), 0, ob.at[:, pl.ds(start, MARGIN), :], row_in.at[1 - side])

    def halo_col_pack(row, n):
        lane, rows = lane_iota(n), pl.ds(row, n)
        re, im = ([ob[comp, rows, blk(0)], ob[comp, rows, blk(1)], ob[comp, rows, pl.ds(256, 32)]] for comp in (0, 1))
        zero = jnp.zeros((n, 96), F32)
        col_s[0, rows, :] = jnp.where(lane < 64, re[0], pltpu.roll(im[0], 64, 1))
        tail = [jnp.where(lane < 32, jnp.concatenate([v[2], zero], 1), v[1]) for v in (re, im)]
        col_s[1, rows, :] = jnp.where(lane < 64, pltpu.roll(tail[0], 16, 1), pltpu.roll(tail[1], 80, 1))

    for row in (0, CORE - MARGIN):
        halo_col_pack(row, MARGIN)
    for a, b in corners:
        send((a, b), 1, col_s.at[b, pl.ds(0 if a == 0 else CORE - MARGIN, MARGIN), :],
             col_in.at[1 - b, pl.ds(CORE + (1 - a) * MARGIN, MARGIN), :])

    @pl.loop(1, CORE // MARGIN - 1)
    def _(i):
        halo_col_pack(pl.multiple_of(i * MARGIN, MARGIN), MARGIN)

    for side in (0, 1):
        send(("col", side), 2, col_s.at[side, :, :], col_in.at[1 - side, pl.ds(0, CORE), :])

    def place_rows(ref, n, first):
        @pl.loop(0, n // MARGIN)
        def _(i):
            at = pl.multiple_of(i * MARGIN, MARGIN)
            rows, to_rows = pl.ds(at, MARGIN), pl.ds(first + at, MARGIN)
            lane = lane_iota(MARGIN)
            for comp in (0, 1):
                a, b = (pltpu.roll(ref[comp, rows, blk(k)], MARGIN, 1) for k in (0, 1))
                c = pltpu.roll(
                    jnp.concatenate([ref[comp, rows, pl.ds(256, 32)], jnp.zeros((MARGIN, 96), F32)], 1), MARGIN, 1)
                cur[comp, to_rows, blk(0)] = jnp.where(lane < MARGIN, 0.0, a)
                cur[comp, to_rows, blk(1)] = jnp.where(lane < MARGIN, a, b)
                cur[comp, to_rows, blk(2)] = jnp.where(lane < MARGIN, b, c)

    place_rows(ob, CORE, MARGIN)

    def halo_col_unpack(side, row, at, n):
        lane, rows = lane_iota(n), pl.ds(row, n)
        strip = col_in[side, pl.ds(at, n), :]
        if side == 0:
            for comp, shift in ((0, 0), (1, 64)):
                new = strip if shift == 0 else pltpu.roll(strip, shift, 1)
                cur[comp, rows, blk(0)] = jnp.where(lane < 48, new, cur[comp, rows, blk(0)])
        else:
            for comp, shift in ((0, 80), (1, 16)):
                cur[comp, rows, blk(2)] = jnp.where(lane >= 80, pltpu.roll(strip, shift, 1), cur[comp, rows, blk(2)])

    @pl.loop(0, TILE // MARGIN)
    def _(i):
        for ref in (ga, gb):
            for comp in (0, 1):
                ref[comp, pl.ds(pl.multiple_of(i * MARGIN, MARGIN), MARGIN), :] = jnp.zeros((MARGIN, TILE), F32)

    loads[1].wait()
    loads[2].wait()
    for copy in loads[3:]:
        copy.wait()
    live_count = cnt[0, 0]

    @pl.loop(0, SLOTS)
    def _(s):
        r, c = off[0, 0, 0, s], off[0, 0, 1, s]
        live = jnp.where(s < live_count, 1.0, 0.0).astype(F32)
        for comp in (0, 1):
            pr[s, comp] = pltpu.roll(pltpu.roll(pb[comp], r, 0), c, 1) * live
        ap[s] = mm(mm(sv[...], ab[0, 0, s]).astype(BF16), sv[...]).astype(BF16)

    def cols_fix(plain, other, lane):
        return jnp.where(lane == 0, other, plain)

    def forward_rows(s, first, buf):
        r, c = off[0, 0, 0, s], off[0, 0, 1, s]
        lane = lane_iota(16)
        hi_c = lane < c
        for at in range(0, HALF, 16):
            m = first + at
            patch = []
            for comp in (0, 1):
                if m < HALF:
                    hi_r = row_iota(16, m) < r
                    three = [
                        jnp.where(hi_r, cur[comp, pl.ds(m + SIDE, 16), blk(b)], cur[comp, pl.ds(m, 16), blk(b)])
                        for b in range(3)
                    ]
                else:
                    three = [cur[comp, pl.ds(m, 16), blk(b)] for b in range(3)]
                patch.append((jnp.where(hi_c, three[2], three[0]), three[1]))
            for b in (0, 1):
                p0, p1 = pr[s, 0, pl.ds(m, 16), blk(b)], pr[s, 1, pl.ds(m, 16), blk(b)]
                xb[buf, pl.ds(at, 16), blk(b)] = (p0 * patch[0][b] - p1 * patch[1][b]).astype(BF16)
                xb[buf, pl.ds(HALF + at, 16), blk(b)] = (p0 * patch[1][b] + p1 * patch[0][b]).astype(BF16)
        v = mm(xb[buf], ttv[...])
        for at in range(0, HALF, 16):
            rows = pl.ds(first + at, 16)
            c_r, s_r = v[at : at + 16, :HALF], v[at : at + 16, HALF:]
            c_i, s_i = v[HALF + at : HALF + at + 16, :HALF], v[HALF + at : HALF + at + 16, HALF:]
            hb[s, rows, blk(0)] = cols_fix(c_r + s_i, c_r, lane).astype(BF16)
            hb[s, rows, blk(1)] = cols_fix(c_r - s_i, s_r, lane).astype(BF16)
            hb[s, rows, blk(2)] = cols_fix(c_i - s_r, c_i, lane).astype(BF16)
            hb[s, rows, blk(3)] = cols_fix(c_i + s_r, s_i, lane).astype(BF16)

    def middle(s, buf):
        u = mm(tv[...], hb[s])
        lane = lane_iota(16)
        for k in range(0, HALF, 16):
            for b in (0, 1):
                lo, hi = slice(k, k + 16), slice(HALF + k, HALF + k + 16)
                re, im = slice(b * HALF, b * HALF + HALF), slice(SIDE + b * HALF, SIDE + b * HALF + HALF)
                c_r, s_r, c_i, s_i = u[lo, re], u[hi, re], u[lo, im], u[hi, im]
                p_r, p_i, m_r, m_i = c_r + s_i, c_i - s_r, c_r - s_i, c_i + s_r
                if k == 0:
                    first = row_iota(16, 0) == 0
                    p_r, p_i = jnp.where(first, c_r, p_r), jnp.where(first, c_i, p_i)
                    m_r, m_i = jnp.where(first, s_r, m_r), jnp.where(first, s_i, m_i)
                f_p = ap[s, pl.ds(k, 16), blk(b)].astype(F32) * lax.rsqrt(p_r * p_r + p_i * p_i + FLOOR) - 1.0
                f_m = ap[s, pl.ds(HALF + k, 16), blk(b)].astype(F32) * lax.rsqrt(m_r * m_r + m_i * m_i + FLOOR) - 1.0
                p_r, p_i, m_r, m_i = p_r * f_p, p_i * f_p, m_r * f_m, m_i * f_m
                a_r, a_i, nb_i, b_r = p_r + m_r, p_i + m_i, m_i - p_i, p_r - m_r
                if k == 0:
                    a_r, a_i = jnp.where(first, p_r, a_r), jnp.where(first, p_i, a_i)
                    nb_i, b_r = jnp.where(first, m_r, nb_i), jnp.where(first, m_i, b_r)
                wb[buf, pl.ds(k, 16), blk(b)] = a_r.astype(BF16)
                wb[buf, pl.ds(k, 16), blk(2 + b)] = a_i.astype(BF16)
                wb[buf, pl.ds(HALF + k, 16), blk(b)] = nb_i.astype(BF16)
                wb[buf, pl.ds(HALF + k, 16), blk(2 + b)] = b_r.astype(BF16)
        y = mm(ttv[...], wb[buf])
        for m in range(0, SIDE, 16):
            rows = slice(m, m + 16)
            p_r, m_r, p_i, m_i = (y[rows, b * HALF : b * HALF + HALF] for b in range(4))
            re = m if m < HALF else HALF + m
            im = re + HALF
            qb[s, pl.ds(re, 16), blk(0)] = cols_fix(p_r + m_r, p_r, lane).astype(BF16)
            qb[s, pl.ds(re, 16), blk(1)] = cols_fix(m_i - p_i, m_r, lane).astype(BF16)
            qb[s, pl.ds(im, 16), blk(0)] = cols_fix(p_i + m_i, p_i, lane).astype(BF16)
            qb[s, pl.ds(im, 16), blk(1)] = cols_fix(p_r - m_r, m_i, lane).astype(BF16)

    def backward_rows(s, first, g):
        products = [mm(qb[slot, pl.ds(2 * first, SIDE), :], tv[...]) for slot in s]
        lane = lane_iota(16)
        for at in range(0, HALF, 16):
            m = first + at
            total = [[None] * 3, [None] * 3]
            below = [[None] * 3, [None] * 3]
            for slot, v in zip(s, products):
                r, c = off[0, 0, 0, slot], off[0, 0, 1, slot]
                terms = ([], [])
                for b in (0, 1):
                    b_r = v[at : at + 16, b * HALF : b * HALF + HALF]
                    b_i = v[HALF + at : HALF + at + 16, b * HALF : b * HALF + HALF]
                    p0, p1 = pr[slot, 0, pl.ds(m, 16), blk(b)], pr[slot, 1, pl.ds(m, 16), blk(b)]
                    terms[0].append(p0 * b_r + p1 * b_i)
                    terms[1].append(p0 * b_i - p1 * b_r)
                for comp in (0, 1):
                    left = terms[comp][0]
                    high = jnp.where(lane < c, left, 0.0)
                    for b, value in enumerate((left - high, terms[comp][1], high)):
                        if m < HALF:
                            low = jnp.where(row_iota(16, m) < r, value, 0.0)
                            value = value - low
                            below[comp][b] = low if below[comp][b] is None else below[comp][b] + low
                        total[comp][b] = value if total[comp][b] is None else total[comp][b] + value
            for comp in (0, 1):
                for b in range(3):
                    g[comp, pl.ds(m, 16), blk(b)] += total[comp][b]
                    if m < HALF:
                        g[comp, pl.ds(m + SIDE, 16), blk(b)] += below[comp][b]

    def forward(first):
        @pl.loop(0, SLOTS // 2)
        def _(i):
            for buf in (0, 1):
                forward_rows(2 * i + buf, first, buf)

    def middles():
        @pl.loop(0, SLOTS // 2)
        def _(i):
            for buf in (0, 1):
                middle(2 * i + buf, buf)

    def backward(first, g):
        @pl.loop(0, SLOTS // 2)
        def _(i):
            backward_rows((2 * i, 2 * i + 1), first, g)

    for side in (0, 1):
        arrived(("col", side), 2, col_s.at[1 - side, :, :], col_in.at[side, pl.ds(0, CORE), :])

        @pl.when(has["col", side])
        def _(side=side):
            @pl.loop(0, CORE // MARGIN)
            def _(i):
                at = pl.multiple_of(i * MARGIN, MARGIN)
                halo_col_unpack(side, MARGIN + at, at, MARGIN)

    forward(INNER)

    for side in (0, 1):
        first = 0 if side == 0 else TILE - MARGIN
        arrived(("row", side), 0, ob.at[:, pl.ds(0, MARGIN), :], row_in.at[side])

        @pl.when(has["row", side])
        def _(side=side, first=first):
            place_rows(row_in.at[side], MARGIN, first)

        @pl.when(jnp.logical_not(has["row", side]))
        def _(first=first):
            for comp in (0, 1):
                cur[comp, pl.ds(first, MARGIN), :] = jnp.zeros((MARGIN, TILE), F32)
    for a, b in corners:
        at = CORE + a * MARGIN
        arrived((a, b), 1, col_s.at[1 - b, pl.ds(0, MARGIN), :], col_in.at[b, pl.ds(at, MARGIN), :])

        @pl.when(peer((a, b))[0])
        def _(a=a, b=b, at=at):
            halo_col_unpack(b, a * (TILE - MARGIN), at, MARGIN)

    forward(EDGE)
    middles()
    backward(EDGE, ga)

    def stage(dst, g, src_row, n_rows):
        for b in range(3):
            for comp in (0, 1):
                dst[b, comp] = g[comp, pl.ds(src_row, n_rows), blk(b)]

    def send_rows(src, dst, kind):
        for side in (0, 1):
            for b in (0, 2):
                send(("row", side), kind + (b,), src.at[side, b], dst.at[1 - side, b])
        for side in (0, 1):
            send(("row", side), kind + (1,), src.at[side, 1], dst.at[1 - side, 1])

    def add_rows(src, dst, kind, g, first, n_rows, blocks):
        for side in (0, 1):
            for b in blocks:
                arrived(("row", side), kind + (b,), src.at[1 - side, b], dst.at[side, b])

            @pl.when(has["row", side])
            def _(side=side):
                for b in blocks:
                    for comp in (0, 1):
                        g[comp, pl.ds(first[side], n_rows), blk(b)] += dst[side, b, comp]

    for side in (0, 1):
        stage(grow_s.at[side], ga, 0 if side == 0 else TILE - WIDE, WIDE)
    send_rows(grow_s, grow_in, ("g",))
    backward(INNER, ga)

    def gcol_index(part):
        first, second = (WIDE, 2 * WIDE) if part == 0 else (0, TILE - WIDE)
        return [(first + j, second + j, j) for j in range(0, WIDE, MARGIN)]

    def gcol_pack(part):
        n = MARGIN
        lane = lane_iota(n)
        base = part * 288
        for row_a, row_b, j in gcol_index(part):
            for side in (0, 1):
                kept = []
                for row, at in ((row_a, j), (row_b, WIDE + j)):
                    re = ga[0, pl.ds(row, n), blk(0 if side == 0 else 2)]
                    im = ga[1, pl.ds(row, n), blk(0 if side == 0 else 2)]
                    if side == 1:
                        strip = jnp.where(lane < 96, pltpu.roll(re, 96, 1), pltpu.roll(im, 64, 1))
                    else:
                        strip = jnp.where(lane < 96, re, pltpu.roll(im, 96, 1))
                    gcol_s[side, pl.ds(base + at, n), :] = strip
                    kept.append(im)
                shift = (96, 32) if side == 0 else (64, 0)
                low = pltpu.roll(kept[0], shift[0], 1)
                high = pltpu.roll(kept[1], shift[1], 1) if shift[1] else kept[1]
                gcol_s[side, pl.ds(base + 192 + j, n), :] = jnp.where(lane < 64, low, high)

    def gcol_unpack(side, part):
        n = MARGIN
        lane = lane_iota(n)
        base = part * 288
        for row_a, row_b, j in gcol_index(part):
            rest = gcol_in[side, pl.ds(base + 192 + j, n), :]
            for row, at, shift in ((row_a, j, 0), (row_b, WIDE + j, 64)):
                strip = gcol_in[side, pl.ds(base + at, n), :]
                if side == 0:
                    re = jnp.where(lane < 96, strip, 0.0)
                    im = jnp.where(lane < 32, pltpu.roll(strip, 32, 1), pltpu.roll(rest, 32 + shift, 1))
                    im = jnp.where(lane < 96, im, 0.0)
                else:
                    re = jnp.where(lane < 32, 0.0, pltpu.roll(strip, 32, 1))
                    tail = pltpu.roll(rest, 64 + shift, 1) if shift == 0 else rest
                    im = jnp.where(lane < 64, pltpu.roll(strip, 64, 1), tail)
                    im = jnp.where(lane < 32, 0.0, im)
                b = 0 if side == 0 else 2
                ga[0, pl.ds(row, n), blk(b)] += re
                ga[1, pl.ds(row, n), blk(b)] += im

    def gcol_send(part):
        rows = pl.ds(part * 288, 288)
        for side in (0, 1):
            send(("col", side), 3 + part, gcol_s.at[side, rows, :], gcol_in.at[1 - side, rows, :])

    def gcol_add(part):
        rows = pl.ds(part * 288, 288)
        for side in (0, 1):
            arrived(("col", side), 3 + part, gcol_s.at[1 - side, rows, :], gcol_in.at[side, rows, :])

            @pl.when(has["col", side])
            def _(side=side):
                gcol_unpack(side, part)

    def update(rows):
        for at in rows:
            lane = lane_iota(MARGIN)
            ok = True
            if at == 0:
                ok = has["row", 0]
            elif at == TILE - MARGIN:
                ok = has["row", 1]
            keep = (
                jnp.logical_and(ok, jnp.logical_or(lane >= MARGIN, has["col", 0])),
                jnp.logical_and(ok, lane >= 0),
                jnp.logical_and(ok, jnp.logical_or(lane < 80, has["col", 1])),
            )
            for comp in (0, 1):
                for b in range(3):
                    cur[comp, pl.ds(at, MARGIN), blk(b)] += jnp.where(
                        keep[b], STEP * ga[comp, pl.ds(at, MARGIN), blk(b)], 0.0)

    gcol_pack(0)
    gcol_send(0)
    gcol_add(0)
    update(range(WIDE, TILE - WIDE, MARGIN))
    forward(INNER)

    first = (0, TILE - WIDE)
    add_rows(grow_s, grow_in, ("g",), ga, first, WIDE, (0, 2))
    gcol_pack(1)
    gcol_send(1)
    add_rows(grow_s, grow_in, ("g",), ga, first, WIDE, (1,))
    gcol_add(1)
    update((0, MARGIN, TILE - WIDE, TILE - MARGIN))

    forward(EDGE)
    middles()
    backward(EDGE, gb)
    for side in (0, 1):
        stage(frow_s.at[side], gb, 0 if side == 0 else TILE - MARGIN, MARGIN)
    send_rows(frow_s, frow_in, ("f",))
    backward(INNER, gb)

    def fcol_index(part):
        if part == 0:
            return [(WIDE + j, j) for j in range(0, 192, MARGIN)]
        return [(MARGIN, 192), (TILE - WIDE, 240)]

    def fcol_pack(part):
        lane = lane_iota(MARGIN)
        for row, at in fcol_index(part):
            rows, to_rows = pl.ds(row, MARGIN), pl.ds(at, MARGIN)
            fcol_s[0, to_rows, :] = jnp.where(
                lane < 64, gb[0, rows, blk(0)], pltpu.roll(gb[1, rows, blk(0)], 64, 1))
            fcol_s[1, to_rows, :] = jnp.where(
                lane < 64, pltpu.roll(gb[0, rows, blk(2)], 48, 1), pltpu.roll(gb[1, rows, blk(2)], 112, 1))

    def fcol_unpack(side, part):
        lane = lane_iota(MARGIN)
        for row, at in fcol_index(part):
            strip = fcol_in[side, pl.ds(at, MARGIN), :]
            if side == 0:
                b, ok = 0, jnp.logical_and(lane >= 48, lane < 96)
                pair = (pltpu.roll(strip, 48, 1), pltpu.roll(strip, 112, 1))
            else:
                b, ok = 2, jnp.logical_and(lane >= 32, lane < 80)
                pair = (pltpu.roll(strip, 32, 1), pltpu.roll(strip, 96, 1))
            for comp in (0, 1):
                gb[comp, pl.ds(row, MARGIN), blk(b)] += jnp.where(ok, pair[comp], 0.0)

    def fcol_send(part):
        rows = pl.ds(*((0, 192), (192, 96))[part])
        for side in (0, 1):
            send(("col", side), 5 + part, fcol_s.at[side, rows, :], fcol_in.at[1 - side, rows, :])

    def fcol_add(part):
        rows = pl.ds(*((0, 192), (192, 96))[part])
        for side in (0, 1):
            arrived(("col", side), 5 + part, fcol_s.at[1 - side, rows, :], fcol_in.at[side, rows, :])

            @pl.when(has["col", side])
            def _(side=side):
                fcol_unpack(side, part)

    def write(row):
        lane, rows, to_rows = lane_iota(MARGIN), pl.ds(row, MARGIN), pl.ds(row - MARGIN, MARGIN)
        for comp in (0, 1):
            v = [pltpu.roll(cur[comp, rows, blk(b)] + STEP * gb[comp, rows, blk(b)], 80, 1) for b in range(3)]
            out[comp, to_rows, blk(0)] = jnp.where(lane < 80, v[0], v[1])
            out[comp, to_rows, blk(1)] = jnp.where(lane < 80, v[1], v[2])
            out[comp, to_rows, pl.ds(256, 32)] = v[2][:, :32]

    fcol_pack(0)
    fcol_send(0)
    fcol_add(0)
    for row in range(WIDE, TILE - WIDE, MARGIN):
        write(row)
    first = (MARGIN, TILE - WIDE)
    add_rows(frow_s, frow_in, ("f",), gb, first, MARGIN, (0, 2))
    fcol_pack(1)
    fcol_send(1)
    add_rows(frow_s, frow_in, ("f",), gb, first, MARGIN, (1,))
    fcol_add(1)
    for row in first:
        write(row)

    for key, kind, src, dst in started:
        @pl.when(peer(key)[0])
        def _(args=(key, kind, src, dst, True)):
            remote(*args).wait_send()


def shards(object_field, probe, amplitudes, offsets, counts):
    table, table_t, swap = (jnp.asarray(a) for a in half_tables())
    anywhere = pl.BlockSpec(memory_space=pl.ANY)
    scalars = pl.BlockSpec(memory_space=pltpu.SMEM)
    v32 = lambda *shape: pltpu.VMEM(shape, F32)
    v16 = lambda *shape: pltpu.VMEM(shape, BF16)
    return pl.pallas_call(
        kernel,
        out_shape=jax.ShapeDtypeStruct(object_field.shape, F32),
        in_specs=[scalars, scalars] + [anywhere] * 6,
        out_specs=pl.BlockSpec(memory_space=pltpu.VMEM),
        scratch_shapes=[
            v32(2, CORE, CORE), v32(2, SIDE, SIDE), v16(1, 1, SLOTS, SIDE, SIDE),
            v16(SIDE, SIDE), v16(SIDE, SIDE), v16(SIDE, SIDE),
            v32(SLOTS, 2, SIDE, SIDE), v16(SLOTS, SIDE, SIDE),
            v16(SLOTS, SIDE, 2 * SIDE), v16(2, SIDE, 2 * SIDE), v16(SLOTS, 2 * SIDE, SIDE), v16(2, SIDE, SIDE),
            v32(2, TILE, TILE), v32(2, TILE, TILE), v32(2, TILE, TILE),
            v32(2, 2, MARGIN, CORE), v32(2, CORE, HALF), v32(2, TILE, HALF),
            v32(2, 3, 2, WIDE, HALF), v32(2, 3, 2, WIDE, HALF),
            v32(2, 576, HALF), v32(2, 576, HALF),
            v32(2, 3, 2, MARGIN, HALF), v32(2, 3, 2, MARGIN, HALF),
            v32(2, CORE, HALF), v32(2, CORE, HALF),
            pltpu.SemaphoreType.DMA((6,)),
            pltpu.SemaphoreType.DMA((28,)),
            pltpu.SemaphoreType.DMA((28,)),
        ],
        compiler_params=pltpu.CompilerParams(
            collective_id=0, has_side_effects=True, vmem_limit_bytes=60 * 1024 * 1024),
        name="ptycho",
    )(jnp.swapaxes(offsets, 2, 3), counts, object_field, probe, amplitudes, table, table_t, swap)


def solution(mesh):
    return jax.shard_map(
        shards,
        mesh=mesh,
        in_specs=(
            P(None, "row", "col"),
            P(),
            P("row", "col", None, None, None),
            P("row", "col", None, None),
            P("row", "col"),
        ),
        out_specs=P(None, "row", "col"),
        check_vma=False,
    )
```

```python
import functools
import math

import jax
import jax.numpy as jnp
import numpy as np
from jax import lax
from jax.experimental import pallas as pl
from jax.experimental.pallas import tpu as pltpu
from jax.sharding import PartitionSpec as P

MARGIN = 48
PASSES = 2
SIDE = 256
HALF = 128
CORE = 288
TILE = 384
SLOTS = 8
STEP = 0.1
FLOOR = 0.01
F32 = jnp.float32
BF16 = jnp.bfloat16

WIDE = 2 * MARGIN

EDGE, INNER = 0, HALF


def half_tables():
    position = np.arange(SIDE)
    angle = (position[:, None] * position[None, :] % SIDE) * (2.0 * math.pi / SIDE)
    scale = 1.0 / math.sqrt(SIDE)
    cosine, sine = np.cos(angle) * scale, np.sin(angle) * scale
    table = np.concatenate([cosine[:HALF], cosine[HALF : HALF + 1], sine[1:HALF]])
    order = np.concatenate([np.arange(HALF), [HALF], np.arange(SIDE - 1, HALF, -1)])
    swap = np.zeros((SIDE, SIDE), np.float32)
    swap[np.arange(SIDE), order] = 1.0
    paired = np.stack([table[:HALF].reshape(8, 16, SIDE), table[HALF:].reshape(8, 16, SIDE)], 1).reshape(SIDE, SIDE)
    return [a.astype(jnp.bfloat16) for a in (table, table.T, paired, swap)]


def mm(a, b):
    return jnp.dot(a, b, preferred_element_type=F32)


def lane_iota(rows):
    return lax.broadcasted_iota(jnp.int32, (rows, HALF), 1)


def row_iota(rows, start):
    return lax.broadcasted_iota(jnp.int32, (rows, HALF), 0) + start


def blk(n):
    return pl.ds(n * HALF, HALF)


def kernel(
    off, cnt, obj, probe, amp, table, table_t, paired, swap, out,
    ob, pb, ab, tv, ttv, tpv, sv,
    pr, ap, hb, wb, qb, xb, cur, ga, gb,
    row_in, tail_s, tail_in, col_s, col_in, grow_s, grow_in, gcol_s, gcol_in, frow_s, frow_in, fcol_s, fcol_in,
    load_sem, send_sem, recv_sem,
):
    n_row, n_col = lax.axis_size("row"), lax.axis_size("col")
    me_r, me_c = lax.axis_index("row"), lax.axis_index("col")
    has = {("row", 0): me_r > 0, ("row", 1): me_r < n_row - 1, ("col", 0): me_c > 0, ("col", 1): me_c < n_col - 1}
    to = {("row", 0): me_r - 1, ("row", 1): me_r + 1, ("col", 0): me_c - 1, ("col", 1): me_c + 1}
    sides = [(axis, side) for axis in ("row", "col") for side in (0, 1)]
    corners = [(a, b) for a in (0, 1) for b in (0, 1)]

    def peer(key):
        if key in has:
            return has[key], {key[0]: to[key]}
        rows, cols = ("row", key[0]), ("col", key[1])
        return jnp.logical_and(has[rows], has[cols]), {"row": to[rows], "col": to[cols]}

    def other(key):
        return (key[0], 1 - key[1]) if key in has else (1 - key[0], 1 - key[1])

    loads = [
        pltpu.make_async_copy(src, dst, load_sem.at[i])
        for i, (src, dst) in enumerate(
            ((obj, ob), (probe, pb), (amp, ab), (table, tv), (table_t, ttv), (paired, tpv), (swap, sv))
        )
    ]
    for copy in loads:
        copy.start()

    barrier = pltpu.get_barrier_semaphore()
    for key in sides + corners:
        ok, device = peer(key)

        @pl.when(ok)
        def _(device=device):
            pl.semaphore_signal(barrier, inc=1, device_id=device, device_id_type=pl.DeviceIdType.MESH)
    kinds, started = {}, []

    def semaphore(kind, key):
        return kinds.setdefault((kind, key), len(kinds))

    def remote(key, kind, src, dst, outgoing):
        here, there = (key, other(key)) if outgoing else (other(key), key)
        return pltpu.make_async_remote_copy(
            src_ref=src, dst_ref=dst,
            send_sem=send_sem.at[semaphore(kind, here)],
            recv_sem=recv_sem.at[semaphore(kind, there)],
            device_id=peer(key)[1],
            device_id_type=pl.DeviceIdType.MESH,
        )

    def send(key, kind, src, dst):
        started.append((key, kind, src, dst))

        @pl.when(peer(key)[0])
        def _():
            remote(key, kind, src, dst, True).start()

    def arrived(key, kind, src, dst):
        @pl.when(peer(key)[0])
        def _():
            remote(key, kind, src, dst, False).wait_recv()

    loads[0].wait()

    def own_rows(ref, comp, rows, n):
        tail = jnp.concatenate([ref[comp, rows, pl.ds(256, 32)], jnp.zeros((n, 96), F32)], 1)
        return ref[comp, rows, blk(0)], ref[comp, rows, blk(1)], tail

    def halo_col_pack(row, n):
        lane, rows = lane_iota(n), pl.ds(row, n)
        re, im = (own_rows(ob, comp, rows, n) for comp in (0, 1))
        col_s[0, rows, :] = jnp.where(lane < 64, re[0], pltpu.roll(im[0], 64, 1))
        tail = [jnp.where(lane < 32, v[2], v[1]) for v in (re, im)]
        col_s[1, rows, :] = jnp.where(lane < 64, pltpu.roll(tail[0], 16, 1), pltpu.roll(tail[1], 80, 1))

    def row_start(side):
        return 0 if side == 0 else CORE - MARGIN

    for side in (0, 1):
        part = [
            pltpu.roll(own_rows(ob, comp, pl.ds(row_start(side) + 24 * h, 24), 24)[2], 32 * (2 * h + comp), 1)
            if h + comp else own_rows(ob, comp, pl.ds(row_start(side), 24), 24)[2]
            for h in (0, 1) for comp in (0, 1)
        ]
        tail_s[side] = part[0] + part[1] + part[2] + part[3]

    @pl.loop(0, CORE // MARGIN)
    def _(i):
        halo_col_pack(pl.multiple_of(i * MARGIN, MARGIN), MARGIN)

    pl.semaphore_wait(barrier, sum(peer(key)[0].astype(jnp.int32) for key in sides + corners))

    for side in (0, 1):
        send(("row", side), 0, ob.at[:, pl.ds(row_start(side), MARGIN), pl.ds(0, SIDE)], row_in.at[1 - side])
        send(("row", side), 7, tail_s.at[side], tail_in.at[1 - side])
    for a, b in corners:
        send((a, b), 1, col_s.at[b, pl.ds(row_start(a), MARGIN), :],
             col_in.at[1 - b, pl.ds(CORE + (1 - a) * MARGIN, MARGIN), :])
    for side in (0, 1):
        send(("col", side), 2, col_s.at[side, :, :], col_in.at[1 - side, pl.ds(0, CORE), :])

    def place(comp, rows, values):
        lane = lane_iota(values[0].shape[0])
        a, b, c = (pltpu.roll(v, MARGIN, 1) for v in values)
        cur[comp, rows, blk(0)] = jnp.where(lane < MARGIN, 0.0, a)
        cur[comp, rows, blk(1)] = jnp.where(lane < MARGIN, a, b)
        cur[comp, rows, blk(2)] = jnp.where(lane < MARGIN, b, c)

    @pl.loop(0, CORE // MARGIN)
    def _(i):
        at = pl.multiple_of(i * MARGIN, MARGIN)
        for comp in (0, 1):
            place(comp, pl.ds(MARGIN + at, MARGIN), own_rows(ob, comp, pl.ds(at, MARGIN), MARGIN))

    def halo_col_unpack(side, row, at, n):
        lane, rows = lane_iota(n), pl.ds(row, n)
        strip = col_in[side, pl.ds(at, n), :]
        if side == 0:
            for comp, shift in ((0, 0), (1, 64)):
                new = strip if shift == 0 else pltpu.roll(strip, shift, 1)
                cur[comp, rows, blk(0)] = jnp.where(lane < 48, new, cur[comp, rows, blk(0)])
        else:
            for comp, shift in ((0, 80), (1, 16)):
                cur[comp, rows, blk(2)] = jnp.where(lane >= 80, pltpu.roll(strip, shift, 1), cur[comp, rows, blk(2)])

    @pl.loop(0, TILE // MARGIN)
    def _(i):
        for ref in (ga, gb):
            for comp in (0, 1):
                ref[comp, pl.ds(pl.multiple_of(i * MARGIN, MARGIN), MARGIN), :] = jnp.zeros((MARGIN, TILE), F32)

    loads[1].wait()
    loads[2].wait()
    for copy in loads[3:]:
        copy.wait()
    live_count = cnt[0, 0]

    @pl.loop(0, SLOTS)
    def _(s):
        r, c = off[0, 0, 0, s], off[0, 0, 1, s]
        live = jnp.where(s < live_count, 1.0, 0.0).astype(F32)
        for comp in (0, 1):
            pr[s, comp] = pltpu.roll(pltpu.roll(pb[comp], r, 0), c, 1) * live
        ap[s] = mm(mm(sv[...], ab[0, 0, s]).astype(BF16), sv[...]).astype(BF16)

    def cols_fix(plain, other, lane):
        return jnp.where(lane == 0, other, plain)

    def forward_rows(s, first, buf):
        r, c = off[0, 0, 0, s], off[0, 0, 1, s]
        lane = lane_iota(16)
        hi_c = lane < c
        for at in range(0, HALF, 16):
            m = first + at
            patch = []
            for comp in (0, 1):
                if m < HALF:
                    hi_r = row_iota(16, m) < r
                    three = [
                        jnp.where(hi_r, cur[comp, pl.ds(m + SIDE, 16), blk(b)], cur[comp, pl.ds(m, 16), blk(b)])
                        for b in range(3)
                    ]
                else:
                    three = [cur[comp, pl.ds(m, 16), blk(b)] for b in range(3)]
                patch.append((jnp.where(hi_c, three[2], three[0]), three[1]))
            for b in (0, 1):
                p0, p1 = pr[s, 0, pl.ds(m, 16), blk(b)], pr[s, 1, pl.ds(m, 16), blk(b)]
                xb[buf, pl.ds(2 * at, 16), blk(b)] = (p0 * patch[0][b] - p1 * patch[1][b]).astype(BF16)
                xb[buf, pl.ds(2 * at + 16, 16), blk(b)] = (p0 * patch[1][b] + p1 * patch[0][b]).astype(BF16)
        v = mm(xb[buf], ttv[...])
        for at in range(0, HALF, 16):
            rows = pl.ds(first + at, 16)
            re, im = slice(2 * at, 2 * at + 16), slice(2 * at + 16, 2 * at + 32)
            c_r, s_r, c_i, s_i = v[re, :HALF], v[re, HALF:], v[im, :HALF], v[im, HALF:]
            hb[s, rows, blk(0)] = cols_fix(c_r + s_i, c_r, lane).astype(BF16)
            hb[s, rows, blk(1)] = cols_fix(c_r - s_i, s_r, lane).astype(BF16)
            hb[s, rows, blk(2)] = cols_fix(c_i - s_r, c_i, lane).astype(BF16)
            hb[s, rows, blk(3)] = cols_fix(c_i + s_r, s_i, lane).astype(BF16)

    def correct(s, buf, u):
        for k in range(0, HALF, 16):
            for b in (0, 1):
                lo, hi = slice(2 * k, 2 * k + 16), slice(2 * k + 16, 2 * k + 32)
                re, im = slice(b * HALF, b * HALF + HALF), slice(SIDE + b * HALF, SIDE + b * HALF + HALF)
                c_r, s_r, c_i, s_i = u[lo, re], u[hi, re], u[lo, im], u[hi, im]
                p_r, p_i, m_r, m_i = c_r + s_i, c_i - s_r, c_r - s_i, c_i + s_r
                if k == 0:
                    first = row_iota(16, 0) == 0
                    p_r, p_i = jnp.where(first, c_r, p_r), jnp.where(first, c_i, p_i)
                    m_r, m_i = jnp.where(first, s_r, m_r), jnp.where(first, s_i, m_i)
                f_p = ap[s, pl.ds(k, 16), blk(b)].astype(F32) * lax.rsqrt(p_r * p_r + p_i * p_i + FLOOR) - 1.0
                f_m = ap[s, pl.ds(HALF + k, 16), blk(b)].astype(F32) * lax.rsqrt(m_r * m_r + m_i * m_i + FLOOR) - 1.0
                p_r, p_i, m_r, m_i = p_r * f_p, p_i * f_p, m_r * f_m, m_i * f_m
                a_r, a_i, nb_i, b_r = p_r + m_r, p_i + m_i, m_i - p_i, p_r - m_r
                if k == 0:
                    a_r, a_i = jnp.where(first, p_r, a_r), jnp.where(first, p_i, a_i)
                    nb_i, b_r = jnp.where(first, m_r, nb_i), jnp.where(first, m_i, b_r)
                wb[buf, pl.ds(k, 16), blk(b)] = a_r.astype(BF16)
                wb[buf, pl.ds(k, 16), blk(2 + b)] = a_i.astype(BF16)
                wb[buf, pl.ds(HALF + k, 16), blk(b)] = nb_i.astype(BF16)
                wb[buf, pl.ds(HALF + k, 16), blk(2 + b)] = b_r.astype(BF16)

    def split_columns(s, y):
        lane = lane_iota(16)
        for m in range(0, SIDE, 16):
            rows = slice(m, m + 16)
            p_r, m_r, p_i, m_i = (y[rows, b * HALF : b * HALF + HALF] for b in range(4))
            re, im = 2 * m, 2 * m + 16
            qb[s, pl.ds(re, 16), blk(0)] = cols_fix(p_r + m_r, p_r, lane).astype(BF16)
            qb[s, pl.ds(re, 16), blk(1)] = cols_fix(m_i - p_i, m_r, lane).astype(BF16)
            qb[s, pl.ds(im, 16), blk(0)] = cols_fix(p_i + m_i, p_i, lane).astype(BF16)
            qb[s, pl.ds(im, 16), blk(1)] = cols_fix(p_r - m_r, m_i, lane).astype(BF16)

    def backward_rows(s, first, g):
        products = [mm(qb[slot, pl.ds(2 * first, SIDE), :], tv[...]) for slot in s]
        lane = lane_iota(16)
        for at in range(0, HALF, 16):
            m = first + at
            total = [[None] * 3, [None] * 3]
            below = [[None] * 3, [None] * 3]
            for slot, v in zip(s, products):
                r, c = off[0, 0, 0, slot], off[0, 0, 1, slot]
                terms = ([], [])
                for b in (0, 1):
                    b_r = v[2 * at : 2 * at + 16, b * HALF : b * HALF + HALF]
                    b_i = v[2 * at + 16 : 2 * at + 32, b * HALF : b * HALF + HALF]
                    p0, p1 = pr[slot, 0, pl.ds(m, 16), blk(b)], pr[slot, 1, pl.ds(m, 16), blk(b)]
                    terms[0].append(p0 * b_r + p1 * b_i)
                    terms[1].append(p0 * b_i - p1 * b_r)
                for comp in (0, 1):
                    left = terms[comp][0]
                    high = jnp.where(lane < c, left, 0.0)
                    for b, value in enumerate((left - high, terms[comp][1], high)):
                        if m < HALF:
                            low = jnp.where(row_iota(16, m) < r, value, 0.0)
                            value = value - low
                            below[comp][b] = low if below[comp][b] is None else below[comp][b] + low
                        total[comp][b] = value if total[comp][b] is None else total[comp][b] + value
            for comp in (0, 1):
                for b in range(3):
                    g[comp, pl.ds(m, 16), blk(b)] += total[comp][b]
                    if m < HALF:
                        g[comp, pl.ds(m + SIDE, 16), blk(b)] += below[comp][b]

    def forward(first):
        @pl.loop(0, SLOTS // 2)
        def _(i):
            for buf in (0, 1):
                forward_rows(2 * i + buf, first, buf)

    def edge_pass(g):
        @pl.loop(0, SLOTS // 2)
        def _(i):
            pair = (2 * i, 2 * i + 1)
            for buf in (0, 1):
                forward_rows(pair[buf], EDGE, buf)
            far = [mm(tpv[...], hb[s]) for s in pair]
            back = []
            for buf in (0, 1):
                correct(pair[buf], buf, far[buf])
                back.append(mm(ttv[...], wb[buf]))
            for buf in (0, 1):
                split_columns(pair[buf], back[buf])
            backward_rows(pair, EDGE, g)

    def backward(first, g):
        @pl.loop(0, SLOTS // 2)
        def _(i):
            backward_rows((2 * i, 2 * i + 1), first, g)

    for side in (0, 1):
        arrived(("col", side), 2, col_s.at[1 - side, :, :], col_in.at[side, pl.ds(0, CORE), :])

        @pl.when(has["col", side])
        def _(side=side):
            @pl.loop(0, CORE // MARGIN)
            def _(i):
                at = pl.multiple_of(i * MARGIN, MARGIN)
                halo_col_unpack(side, MARGIN + at, at, MARGIN)

    forward(INNER)

    for side in (0, 1):
        first = 0 if side == 0 else TILE - MARGIN
        arrived(("row", side), 0, ob.at[:, pl.ds(0, MARGIN), pl.ds(0, SIDE)], row_in.at[side])
        arrived(("row", side), 7, tail_s.at[1 - side], tail_in.at[side])

        @pl.when(has["row", side])
        def _(side=side, first=first):
            lane = lane_iota(24)
            for h in (0, 1):
                for comp in (0, 1):
                    shift = (HALF - 32 * (2 * h + comp)) % HALF
                    tail = tail_in[side] if shift == 0 else pltpu.roll(tail_in[side], shift, 1)
                    rows = pl.ds(24 * h, 24)
                    place(comp, pl.ds(first + 24 * h, 24),
                          (row_in[side, comp, rows, blk(0)], row_in[side, comp, rows, blk(1)],
                           jnp.where(lane < 32, tail, 0.0)))

        @pl.when(jnp.logical_not(has["row", side]))
        def _(first=first):
            for comp in (0, 1):
                cur[comp, pl.ds(first, MARGIN), :] = jnp.zeros((MARGIN, TILE), F32)
    for a, b in corners:
        at = CORE + a * MARGIN
        arrived((a, b), 1, col_s.at[1 - b, pl.ds(0, MARGIN), :], col_in.at[b, pl.ds(at, MARGIN), :])

        @pl.when(peer((a, b))[0])
        def _(a=a, b=b, at=at):
            halo_col_unpack(b, a * (TILE - MARGIN), at, MARGIN)

    edge_pass(ga)

    def stage(dst, g, src_row, n_rows):
        for b in range(3):
            for comp in (0, 1):
                dst[b, comp] = g[comp, pl.ds(src_row, n_rows), blk(b)]

    def send_rows(src, dst, kind):
        for side in (0, 1):
            for b in (0, 2):
                send(("row", side), kind + (b,), src.at[side, b], dst.at[1 - side, b])
        for side in (0, 1):
            send(("row", side), kind + (1,), src.at[side, 1], dst.at[1 - side, 1])

    def add_rows(src, dst, kind, g, first, n_rows, blocks):
        for side in (0, 1):
            for b in blocks:
                arrived(("row", side), kind + (b,), src.at[1 - side, b], dst.at[side, b])

            @pl.when(has["row", side])
            def _(side=side):
                for b in blocks:
                    for comp in (0, 1):
                        g[comp, pl.ds(first[side], n_rows), blk(b)] += dst[side, b, comp]

    for side in (0, 1):
        stage(grow_s.at[side], ga, 0 if side == 0 else TILE - WIDE, WIDE)
    send_rows(grow_s, grow_in, ("g",))
    backward(INNER, ga)

    def gcol_index(part):
        first, second = (WIDE, 2 * WIDE) if part == 0 else (0, TILE - WIDE)
        return [(first + j, second + j, j) for j in range(0, WIDE, MARGIN)]

    def gcol_pack(part):
        n = MARGIN
        lane = lane_iota(n)
        base = part * 288
        for row_a, row_b, j in gcol_index(part):
            for side in (0, 1):
                kept = []
                for row, at in ((row_a, j), (row_b, WIDE + j)):
                    re = ga[0, pl.ds(row, n), blk(0 if side == 0 else 2)]
                    im = ga[1, pl.ds(row, n), blk(0 if side == 0 else 2)]
                    if side == 1:
                        strip = jnp.where(lane < 96, pltpu.roll(re, 96, 1), pltpu.roll(im, 64, 1))
                    else:
                        strip = jnp.where(lane < 96, re, pltpu.roll(im, 96, 1))
                    gcol_s[side, pl.ds(base + at, n), :] = strip
                    kept.append(im)
                shift = (96, 32) if side == 0 else (64, 0)
                low = pltpu.roll(kept[0], shift[0], 1)
                high = pltpu.roll(kept[1], shift[1], 1) if shift[1] else kept[1]
                gcol_s[side, pl.ds(base + 192 + j, n), :] = jnp.where(lane < 64, low, high)

    def gcol_unpack(side, part):
        n = MARGIN
        lane = lane_iota(n)
        base = part * 288
        for row_a, row_b, j in gcol_index(part):
            rest = gcol_in[side, pl.ds(base + 192 + j, n), :]
            for row, at, shift in ((row_a, j, 0), (row_b, WIDE + j, 64)):
                strip = gcol_in[side, pl.ds(base + at, n), :]
                if side == 0:
                    re = jnp.where(lane < 96, strip, 0.0)
                    im = jnp.where(lane < 32, pltpu.roll(strip, 32, 1), pltpu.roll(rest, 32 + shift, 1))
                    im = jnp.where(lane < 96, im, 0.0)
                else:
                    re = jnp.where(lane < 32, 0.0, pltpu.roll(strip, 32, 1))
                    tail = pltpu.roll(rest, 64 + shift, 1) if shift == 0 else rest
                    im = jnp.where(lane < 64, pltpu.roll(strip, 64, 1), tail)
                    im = jnp.where(lane < 32, 0.0, im)
                b = 0 if side == 0 else 2
                ga[0, pl.ds(row, n), blk(b)] += re
                ga[1, pl.ds(row, n), blk(b)] += im

    def gcol_send(part):
        rows = pl.ds(part * 288, 288)
        for side in (0, 1):
            send(("col", side), 3 + part, gcol_s.at[side, rows, :], gcol_in.at[1 - side, rows, :])

    def gcol_add(part):
        rows = pl.ds(part * 288, 288)
        for side in (0, 1):
            arrived(("col", side), 3 + part, gcol_s.at[1 - side, rows, :], gcol_in.at[side, rows, :])

            @pl.when(has["col", side])
            def _(side=side):
                gcol_unpack(side, part)

    def update(rows):
        for at in rows:
            lane = lane_iota(MARGIN)
            ok = True
            if at == 0:
                ok = has["row", 0]
            elif at == TILE - MARGIN:
                ok = has["row", 1]
            keep = (
                jnp.logical_and(ok, jnp.logical_or(lane >= MARGIN, has["col", 0])),
                jnp.logical_and(ok, lane >= 0),
                jnp.logical_and(ok, jnp.logical_or(lane < 80, has["col", 1])),
            )
            for comp in (0, 1):
                for b in range(3):
                    cur[comp, pl.ds(at, MARGIN), blk(b)] += jnp.where(
                        keep[b], STEP * ga[comp, pl.ds(at, MARGIN), blk(b)], 0.0)

    gcol_pack(0)
    gcol_send(0)
    gcol_add(0)
    update(range(WIDE, TILE - WIDE, MARGIN))
    forward(INNER)

    first = (0, TILE - WIDE)
    add_rows(grow_s, grow_in, ("g",), ga, first, WIDE, (0, 2))
    gcol_pack(1)
    gcol_send(1)
    add_rows(grow_s, grow_in, ("g",), ga, first, WIDE, (1,))
    gcol_add(1)
    update((0, MARGIN, TILE - WIDE, TILE - MARGIN))

    edge_pass(gb)
    for side in (0, 1):
        stage(frow_s.at[side], gb, 0 if side == 0 else TILE - MARGIN, MARGIN)
    send_rows(frow_s, frow_in, ("f",))
    backward(INNER, gb)

    def fcol_index(part):
        if part == 0:
            return [(WIDE + j, j) for j in range(0, 192, MARGIN)]
        return [(MARGIN, 192), (TILE - WIDE, 240)]

    def fcol_pack(part):
        lane = lane_iota(MARGIN)
        for row, at in fcol_index(part):
            rows, to_rows = pl.ds(row, MARGIN), pl.ds(at, MARGIN)
            fcol_s[0, to_rows, :] = jnp.where(
                lane < 64, gb[0, rows, blk(0)], pltpu.roll(gb[1, rows, blk(0)], 64, 1))
            fcol_s[1, to_rows, :] = jnp.where(
                lane < 64, pltpu.roll(gb[0, rows, blk(2)], 48, 1), pltpu.roll(gb[1, rows, blk(2)], 112, 1))

    def fcol_unpack(side, part):
        lane = lane_iota(MARGIN)
        for row, at in fcol_index(part):
            strip = fcol_in[side, pl.ds(at, MARGIN), :]
            if side == 0:
                b, ok = 0, jnp.logical_and(lane >= 48, lane < 96)
                pair = (pltpu.roll(strip, 48, 1), pltpu.roll(strip, 112, 1))
            else:
                b, ok = 2, jnp.logical_and(lane >= 32, lane < 80)
                pair = (pltpu.roll(strip, 32, 1), pltpu.roll(strip, 96, 1))
            for comp in (0, 1):
                gb[comp, pl.ds(row, MARGIN), blk(b)] += jnp.where(ok, pair[comp], 0.0)

    def fcol_send(part):
        rows = pl.ds(*((0, 192), (192, 96))[part])
        for side in (0, 1):
            send(("col", side), 5 + part, fcol_s.at[side, rows, :], fcol_in.at[1 - side, rows, :])

    def fcol_add(part):
        rows = pl.ds(*((0, 192), (192, 96))[part])
        for side in (0, 1):
            arrived(("col", side), 5 + part, fcol_s.at[1 - side, rows, :], fcol_in.at[side, rows, :])

            @pl.when(has["col", side])
            def _(side=side):
                fcol_unpack(side, part)

    def write(row):
        lane, rows, to_rows = lane_iota(MARGIN), pl.ds(row, MARGIN), pl.ds(row - MARGIN, MARGIN)
        for comp in (0, 1):
            v = [pltpu.roll(cur[comp, rows, blk(b)] + STEP * gb[comp, rows, blk(b)], 80, 1) for b in range(3)]
            out[comp, to_rows, blk(0)] = jnp.where(lane < 80, v[0], v[1])
            out[comp, to_rows, blk(1)] = jnp.where(lane < 80, v[1], v[2])
            out[comp, to_rows, pl.ds(256, 32)] = v[2][:, :32]

    fcol_pack(0)
    fcol_send(0)
    fcol_add(0)
    for row in range(WIDE, TILE - WIDE, MARGIN):
        write(row)
    first = (MARGIN, TILE - WIDE)
    add_rows(frow_s, frow_in, ("f",), gb, first, MARGIN, (0, 2))
    fcol_pack(1)
    fcol_send(1)
    add_rows(frow_s, frow_in, ("f",), gb, first, MARGIN, (1,))
    fcol_add(1)
    for row in first:
        write(row)

    for key, kind, src, dst in started:
        @pl.when(peer(key)[0])
        def _(args=(key, kind, src, dst, True)):
            remote(*args).wait_send()


def shards(object_field, probe, amplitudes, offsets, counts):
    tables = (jnp.asarray(a) for a in half_tables())
    anywhere = pl.BlockSpec(memory_space=pl.ANY)
    scalars = pl.BlockSpec(memory_space=pltpu.SMEM)
    v32 = lambda *shape: pltpu.VMEM(shape, F32)
    v16 = lambda *shape: pltpu.VMEM(shape, BF16)
    return pl.pallas_call(
        kernel,
        out_shape=jax.ShapeDtypeStruct(object_field.shape, F32),
        in_specs=[scalars, scalars] + [anywhere] * 7,
        out_specs=pl.BlockSpec(memory_space=pltpu.VMEM),
        scratch_shapes=[
            v32(2, CORE, CORE), v32(2, SIDE, SIDE), v16(1, 1, SLOTS, SIDE, SIDE),
            v16(SIDE, SIDE), v16(SIDE, SIDE), v16(SIDE, SIDE), v16(SIDE, SIDE),
            v32(SLOTS, 2, SIDE, SIDE), v16(SLOTS, SIDE, SIDE),
            v16(SLOTS, SIDE, 2 * SIDE), v16(2, SIDE, 2 * SIDE), v16(SLOTS, 2 * SIDE, SIDE), v16(2, SIDE, SIDE),
            v32(2, TILE, TILE), v32(2, TILE, TILE), v32(2, TILE, TILE),
            v32(2, 2, MARGIN, SIDE), v32(2, MARGIN // 2, HALF), v32(2, MARGIN // 2, HALF), v32(2, CORE, HALF), v32(2, TILE, HALF),
            v32(2, 3, 2, WIDE, HALF), v32(2, 3, 2, WIDE, HALF),
            v32(2, 576, HALF), v32(2, 576, HALF),
            v32(2, 3, 2, MARGIN, HALF), v32(2, 3, 2, MARGIN, HALF),
            v32(2, CORE, HALF), v32(2, CORE, HALF),
            pltpu.SemaphoreType.DMA((7,)),
            pltpu.SemaphoreType.DMA((30,)),
            pltpu.SemaphoreType.DMA((30,)),
        ],
        compiler_params=pltpu.CompilerParams(
            collective_id=0, has_side_effects=True, vmem_limit_bytes=60 * 1024 * 1024),
        name="ptycho",
    )(jnp.swapaxes(offsets, 2, 3), counts, object_field, probe, amplitudes, *tables)


def solution(mesh):
    return jax.shard_map(
        shards,
        mesh=mesh,
        in_specs=(
            P(None, "row", "col"),
            P(),
            P("row", "col", None, None, None),
            P("row", "col", None, None),
            P("row", "col"),
        ),
        out_specs=P(None, "row", "col"),
        check_vma=False,
    )
```

```python
import functools
import math

import jax
import jax.numpy as jnp
import numpy as np
from jax import lax
from jax.experimental import pallas as pl
from jax.experimental.pallas import tpu as pltpu
from jax.sharding import PartitionSpec as P

MARGIN = 48
PASSES = 2
SIDE = 256
HALF = 128
CORE = 288
TILE = 384
SLOTS = 8
STEP = 0.1
FLOOR = 0.01
F32 = jnp.float32
BF16 = jnp.bfloat16

WIDE = 2 * MARGIN
QUARTER = CORE // 4

EDGE, INNER = 0, HALF


def half_tables():
    position = np.arange(SIDE)
    angle = (position[:, None] * position[None, :] % SIDE) * (2.0 * math.pi / SIDE)
    scale = 1.0 / math.sqrt(SIDE)
    cosine, sine = np.cos(angle) * scale, np.sin(angle) * scale
    table = np.concatenate([cosine[:HALF], cosine[HALF : HALF + 1], sine[1:HALF]])
    order = np.concatenate([np.arange(HALF), [HALF], np.arange(SIDE - 1, HALF, -1)])
    swap = np.zeros((SIDE, SIDE), np.float32)
    swap[np.arange(SIDE), order] = 1.0
    paired = np.stack([table[:HALF].reshape(8, 16, SIDE), table[HALF:].reshape(8, 16, SIDE)], 1).reshape(SIDE, SIDE)
    return [a.astype(jnp.bfloat16) for a in (table, table.T, paired, swap)]


def mm(a, b):
    return jnp.dot(a, b, preferred_element_type=F32)


def lane_iota(rows):
    return lax.broadcasted_iota(jnp.int32, (rows, HALF), 1)


def row_iota(rows, start):
    return lax.broadcasted_iota(jnp.int32, (rows, HALF), 0) + start


def blk(n):
    return pl.ds(n * HALF, HALF)


def kernel(
    off, cnt, obj, probe, amp, table, table_t, paired, swap, out,
    ob, pb, ab, tv, ttv, tpv, sv,
    pr, ap, hb, wb, qb, xb, cur, ga, gb,
    row_in, tail_s, tail_in, col_s, col_in, corner_s, corner_in, grow_s, grow_in, gcol_s, gcol_in, frow_s, frow_in, fcol_s, fcol_in,
    load_sem, send_sem, recv_sem,
):
    n_row, n_col = lax.axis_size("row"), lax.axis_size("col")
    me_r, me_c = lax.axis_index("row"), lax.axis_index("col")
    has = {("row", 0): me_r > 0, ("row", 1): me_r < n_row - 1, ("col", 0): me_c > 0, ("col", 1): me_c < n_col - 1}
    to = {("row", 0): me_r - 1, ("row", 1): me_r + 1, ("col", 0): me_c - 1, ("col", 1): me_c + 1}
    sides = [(axis, side) for axis in ("row", "col") for side in (0, 1)]
    corners = [(a, b) for a in (0, 1) for b in (0, 1)]

    def peer(key):
        if key in has:
            return has[key], {key[0]: to[key]}
        rows, cols = ("row", key[0]), ("col", key[1])
        return jnp.logical_and(has[rows], has[cols]), {"row": to[rows], "col": to[cols]}

    def other(key):
        return (key[0], 1 - key[1]) if key in has else (1 - key[0], 1 - key[1])

    loads = [
        pltpu.make_async_copy(src, dst, load_sem.at[i])
        for i, (src, dst) in enumerate(
            ((obj, ob), (probe, pb), (amp, ab), (table, tv), (table_t, ttv), (paired, tpv), (swap, sv))
        )
    ]
    for copy in loads:
        copy.start()

    barrier = pltpu.get_barrier_semaphore()
    for key in sides + corners:
        ok, device = peer(key)

        @pl.when(ok)
        def _(device=device):
            pl.semaphore_signal(barrier, inc=1, device_id=device, device_id_type=pl.DeviceIdType.MESH)
    kinds, started = {}, []

    def semaphore(kind, key):
        return kinds.setdefault((kind, key), len(kinds))

    def remote(key, kind, src, dst, outgoing):
        here, there = (key, other(key)) if outgoing else (other(key), key)
        return pltpu.make_async_remote_copy(
            src_ref=src, dst_ref=dst,
            send_sem=send_sem.at[semaphore(kind, here)],
            recv_sem=recv_sem.at[semaphore(kind, there)],
            device_id=peer(key)[1],
            device_id_type=pl.DeviceIdType.MESH,
        )

    def send(key, kind, src, dst):
        started.append((key, kind, src, dst))

        @pl.when(peer(key)[0])
        def _():
            remote(key, kind, src, dst, True).start()

    def arrived(key, kind, src, dst):
        @pl.when(peer(key)[0])
        def _():
            remote(key, kind, src, dst, False).wait_recv()

    loads[0].wait()

    def own_rows(ref, comp, rows, n):
        tail = jnp.concatenate([ref[comp, rows, pl.ds(256, 32)], jnp.zeros((n, 96), F32)], 1)
        return ref[comp, rows, blk(0)], ref[comp, rows, blk(1)], tail

    def rolled(value, shift):
        return pltpu.roll(value, shift % HALF, 1) if shift % HALF else value

    def pack(dst, base, strips):
        n = strips[0].shape[0]
        lane = lane_iota(n)
        for k in range(3):
            dst[pl.ds(base + k * n, n), :] = jnp.where(lane < 96, strips[k], rolled(strips[3], 96 - 32 * k))

    def unpack(src, base, n):
        lane = lane_iota(n)
        three = [src[pl.ds(base + k * n, n), :] for k in range(3)]
        a, b, c = (rolled(v, 32 * k + 32) for k, v in enumerate(three))
        return three + [jnp.where(lane < 32, a, jnp.where(lane < 64, b, c))]

    def pair_up(re, im, at):
        return jnp.where(lane_iota(re.shape[0]) < MARGIN, rolled(re, -at), rolled(im, MARGIN - at))

    def own_strip(side, row, n):
        re, im = (own_rows(ob, comp, pl.ds(row, n), n) for comp in (0, 1))
        if side == 0:
            return pair_up(re[0], im[0], 0)
        lane = lane_iota(n)
        return pair_up(*(jnp.where(lane < 32, v[2], v[1]) for v in (re, im)), 112)

    def row_start(side):
        return 0 if side == 0 else CORE - MARGIN

    for side in (0, 1):
        part = [
            pltpu.roll(own_rows(ob, comp, pl.ds(row_start(side) + 24 * h, 24), 24)[2], 32 * (2 * h + comp), 1)
            if h + comp else own_rows(ob, comp, pl.ds(row_start(side), 24), 24)[2]
            for h in (0, 1) for comp in (0, 1)
        ]
        tail_s[side] = part[0] + part[1] + part[2] + part[3]

    for b in (0, 1):
        for a in (0, 1):
            corner_s[b, a] = own_strip(b, row_start(a), MARGIN)
        pack(col_s.at[b], 0, [own_strip(b, k * QUARTER, QUARTER) for k in range(4)])

    pl.semaphore_wait(barrier, sum(peer(key)[0].astype(jnp.int32) for key in sides + corners))

    for side in (0, 1):
        send(("row", side), 0, ob.at[:, pl.ds(row_start(side), MARGIN), pl.ds(0, SIDE)], row_in.at[1 - side])
        send(("row", side), 7, tail_s.at[side], tail_in.at[1 - side])
    for a, b in corners:
        send((a, b), 1, corner_s.at[b, a], corner_in.at[1 - b, 1 - a])
    for side in (0, 1):
        send(("col", side), 2, col_s.at[side], col_in.at[1 - side])

    def place(comp, rows, values):
        lane = lane_iota(values[0].shape[0])
        a, b, c = (pltpu.roll(v, MARGIN, 1) for v in values)
        cur[comp, rows, blk(0)] = jnp.where(lane < MARGIN, 0.0, a)
        cur[comp, rows, blk(1)] = jnp.where(lane < MARGIN, a, b)
        cur[comp, rows, blk(2)] = jnp.where(lane < MARGIN, b, c)

    @pl.loop(0, CORE // MARGIN)
    def _(i):
        at = pl.multiple_of(i * MARGIN, MARGIN)
        for comp in (0, 1):
            place(comp, pl.ds(MARGIN + at, MARGIN), own_rows(ob, comp, pl.ds(at, MARGIN), MARGIN))

    def place_columns(side, row, strip):
        n = strip.shape[0]
        lane, rows = lane_iota(n), pl.ds(row, n)
        for comp in (0, 1):
            if side == 0:
                new = rolled(strip, -MARGIN * comp)
                cur[comp, rows, blk(0)] = jnp.where(lane < MARGIN, new, cur[comp, rows, blk(0)])
            else:
                new = rolled(strip, 80 - MARGIN * comp)
                cur[comp, rows, blk(2)] = jnp.where(lane >= 80, new, cur[comp, rows, blk(2)])

    @pl.loop(0, TILE // MARGIN)
    def _(i):
        for ref in (ga, gb):
            for comp in (0, 1):
                ref[comp, pl.ds(pl.multiple_of(i * MARGIN, MARGIN), MARGIN), :] = jnp.zeros((MARGIN, TILE), F32)

    loads[1].wait()
    loads[2].wait()
    for copy in loads[3:]:
        copy.wait()
    live_count = cnt[0, 0]

    @pl.loop(0, SLOTS)
    def _(s):
        r, c = off[0, 0, 0, s], off[0, 0, 1, s]
        live = jnp.where(s < live_count, 1.0, 0.0).astype(F32)
        for comp in (0, 1):
            pr[s, comp] = pltpu.roll(pltpu.roll(pb[comp], r, 0), c, 1) * live
        ap[s] = mm(mm(sv[...], ab[0, 0, s]).astype(BF16), sv[...])

    def cols_fix(plain, other, lane):
        return jnp.where(lane == 0, other, plain)

    def forward_rows(s, first, buf):
        r, c = off[0, 0, 0, s], off[0, 0, 1, s]
        lane = lane_iota(16)
        hi_c = lane < c
        for at in range(0, HALF, 16):
            m = first + at
            patch = []
            for comp in (0, 1):
                if m < HALF:
                    hi_r = row_iota(16, m) < r
                    three = [
                        jnp.where(hi_r, cur[comp, pl.ds(m + SIDE, 16), blk(b)], cur[comp, pl.ds(m, 16), blk(b)])
                        for b in range(3)
                    ]
                else:
                    three = [cur[comp, pl.ds(m, 16), blk(b)] for b in range(3)]
                patch.append((jnp.where(hi_c, three[2], three[0]), three[1]))
            for b in (0, 1):
                p0, p1 = pr[s, 0, pl.ds(m, 16), blk(b)], pr[s, 1, pl.ds(m, 16), blk(b)]
                xb[buf, pl.ds(2 * at, 16), blk(b)] = (p0 * patch[0][b] - p1 * patch[1][b]).astype(BF16)
                xb[buf, pl.ds(2 * at + 16, 16), blk(b)] = (p0 * patch[1][b] + p1 * patch[0][b]).astype(BF16)
        v = mm(xb[buf], ttv[...])
        for at in range(0, HALF, 16):
            rows = pl.ds(first + at, 16)
            re, im = slice(2 * at, 2 * at + 16), slice(2 * at + 16, 2 * at + 32)
            c_r, s_r, c_i, s_i = v[re, :HALF], v[re, HALF:], v[im, :HALF], v[im, HALF:]
            hb[s, rows, blk(0)] = cols_fix(c_r + s_i, c_r, lane).astype(BF16)
            hb[s, rows, blk(1)] = cols_fix(c_r - s_i, s_r, lane).astype(BF16)
            hb[s, rows, blk(2)] = cols_fix(c_i - s_r, c_i, lane).astype(BF16)
            hb[s, rows, blk(3)] = cols_fix(c_i + s_r, s_i, lane).astype(BF16)

    def correct(s, buf, u):
        for k in range(0, HALF, 16):
            for b in (0, 1):
                lo, hi = slice(2 * k, 2 * k + 16), slice(2 * k + 16, 2 * k + 32)
                re, im = slice(b * HALF, b * HALF + HALF), slice(SIDE + b * HALF, SIDE + b * HALF + HALF)
                c_r, s_r, c_i, s_i = u[lo, re], u[hi, re], u[lo, im], u[hi, im]
                p_r, p_i, m_r, m_i = c_r + s_i, c_i - s_r, c_r - s_i, c_i + s_r
                if k == 0:
                    first = row_iota(16, 0) == 0
                    p_r, p_i = jnp.where(first, c_r, p_r), jnp.where(first, c_i, p_i)
                    m_r, m_i = jnp.where(first, s_r, m_r), jnp.where(first, s_i, m_i)
                f_p = ap[s, pl.ds(k, 16), blk(b)] * lax.rsqrt(p_r * p_r + p_i * p_i + FLOOR) - 1.0
                f_m = ap[s, pl.ds(HALF + k, 16), blk(b)] * lax.rsqrt(m_r * m_r + m_i * m_i + FLOOR) - 1.0
                p_r, p_i, m_r, m_i = p_r * f_p, p_i * f_p, m_r * f_m, m_i * f_m
                a_r, a_i, nb_i, b_r = p_r + m_r, p_i + m_i, m_i - p_i, p_r - m_r
                if k == 0:
                    a_r, a_i = jnp.where(first, p_r, a_r), jnp.where(first, p_i, a_i)
                    nb_i, b_r = jnp.where(first, m_r, nb_i), jnp.where(first, m_i, b_r)
                wb[buf, pl.ds(k, 16), blk(b)] = a_r.astype(BF16)
                wb[buf, pl.ds(k, 16), blk(2 + b)] = a_i.astype(BF16)
                wb[buf, pl.ds(HALF + k, 16), blk(b)] = nb_i.astype(BF16)
                wb[buf, pl.ds(HALF + k, 16), blk(2 + b)] = b_r.astype(BF16)

    def split_columns(s, y):
        lane = lane_iota(16)
        for m in range(0, SIDE, 16):
            rows = slice(m, m + 16)
            p_r, m_r, p_i, m_i = (y[rows, b * HALF : b * HALF + HALF] for b in range(4))
            re, im = 2 * m, 2 * m + 16
            qb[s, pl.ds(re, 16), blk(0)] = cols_fix(p_r + m_r, p_r, lane).astype(BF16)
            qb[s, pl.ds(re, 16), blk(1)] = cols_fix(m_i - p_i, m_r, lane).astype(BF16)
            qb[s, pl.ds(im, 16), blk(0)] = cols_fix(p_i + m_i, p_i, lane).astype(BF16)
            qb[s, pl.ds(im, 16), blk(1)] = cols_fix(p_r - m_r, m_i, lane).astype(BF16)

    def backward_rows(s, first, g):
        products = [mm(qb[slot, pl.ds(2 * first, SIDE), :], tv[...]) for slot in s]
        lane = lane_iota(16)
        for at in range(0, HALF, 16):
            m = first + at
            total = [[None] * 3, [None] * 3]
            below = [[None] * 3, [None] * 3]
            for slot, v in zip(s, products):
                r, c = off[0, 0, 0, slot], off[0, 0, 1, slot]
                terms = ([], [])
                for b in (0, 1):
                    b_r = v[2 * at : 2 * at + 16, b * HALF : b * HALF + HALF]
                    b_i = v[2 * at + 16 : 2 * at + 32, b * HALF : b * HALF + HALF]
                    p0, p1 = pr[slot, 0, pl.ds(m, 16), blk(b)], pr[slot, 1, pl.ds(m, 16), blk(b)]
                    terms[0].append(p0 * b_r + p1 * b_i)
                    terms[1].append(p0 * b_i - p1 * b_r)
                for comp in (0, 1):
                    left = terms[comp][0]
                    high = jnp.where(lane < c, left, 0.0)
                    for b, value in enumerate((left - high, terms[comp][1], high)):
                        if m < HALF:
                            low = jnp.where(row_iota(16, m) < r, value, 0.0)
                            value = value - low
                            below[comp][b] = low if below[comp][b] is None else below[comp][b] + low
                        total[comp][b] = value if total[comp][b] is None else total[comp][b] + value
            for comp in (0, 1):
                for b in range(3):
                    g[comp, pl.ds(m, 16), blk(b)] += total[comp][b]
                    if m < HALF:
                        g[comp, pl.ds(m + SIDE, 16), blk(b)] += below[comp][b]

    def forward(first):
        @pl.loop(0, SLOTS // 2)
        def _(i):
            for buf in (0, 1):
                forward_rows(2 * i + buf, first, buf)

    def edge_pass(g):
        @pl.loop(0, SLOTS // 2)
        def _(i):
            pair = (2 * i, 2 * i + 1)
            for buf in (0, 1):
                forward_rows(pair[buf], EDGE, buf)
            far = [mm(tpv[...], hb[s]) for s in pair]
            back = []
            for buf in (0, 1):
                correct(pair[buf], buf, far[buf])
                back.append(mm(ttv[...], wb[buf]))
            for buf in (0, 1):
                split_columns(pair[buf], back[buf])
            backward_rows(pair, EDGE, g)

    def backward(first, g):
        @pl.loop(0, SLOTS // 2)
        def _(i):
            backward_rows((2 * i, 2 * i + 1), first, g)

    for side in (0, 1):
        arrived(("col", side), 2, col_s.at[1 - side], col_in.at[side])

        @pl.when(has["col", side])
        def _(side=side):
            for k, strip in enumerate(unpack(col_in.at[side], 0, QUARTER)):
                place_columns(side, MARGIN + k * QUARTER, strip)

    forward(INNER)

    for side in (0, 1):
        first = 0 if side == 0 else TILE - MARGIN
        arrived(("row", side), 0, ob.at[:, pl.ds(0, MARGIN), pl.ds(0, SIDE)], row_in.at[side])
        arrived(("row", side), 7, tail_s.at[1 - side], tail_in.at[side])

        @pl.when(has["row", side])
        def _(side=side, first=first):
            lane = lane_iota(24)
            for h in (0, 1):
                for comp in (0, 1):
                    shift = (HALF - 32 * (2 * h + comp)) % HALF
                    tail = tail_in[side] if shift == 0 else pltpu.roll(tail_in[side], shift, 1)
                    rows = pl.ds(24 * h, 24)
                    place(comp, pl.ds(first + 24 * h, 24),
                          (row_in[side, comp, rows, blk(0)], row_in[side, comp, rows, blk(1)],
                           jnp.where(lane < 32, tail, 0.0)))

        @pl.when(jnp.logical_not(has["row", side]))
        def _(first=first):
            for comp in (0, 1):
                cur[comp, pl.ds(first, MARGIN), :] = jnp.zeros((MARGIN, TILE), F32)
    for a, b in corners:
        arrived((a, b), 1, corner_s.at[1 - b, 1 - a], corner_in.at[b, a])

        @pl.when(peer((a, b))[0])
        def _(a=a, b=b):
            place_columns(b, a * (TILE - MARGIN), corner_in[b, a])

    edge_pass(ga)

    def stage(dst, g, src_row, n_rows):
        for b in range(3):
            for comp in (0, 1):
                dst[b, comp] = g[comp, pl.ds(src_row, n_rows), blk(b)]

    def send_rows(src, dst, kind):
        for side in (0, 1):
            for b in (0, 2):
                send(("row", side), kind + (b,), src.at[side, b], dst.at[1 - side, b])
        for side in (0, 1):
            send(("row", side), kind + (1,), src.at[side, 1], dst.at[1 - side, 1])

    def add_rows(src, dst, kind, g, first, n_rows, blocks):
        for side in (0, 1):
            for b in blocks:
                arrived(("row", side), kind + (b,), src.at[1 - side, b], dst.at[side, b])

            @pl.when(has["row", side])
            def _(side=side):
                for b in blocks:
                    for comp in (0, 1):
                        g[comp, pl.ds(first[side], n_rows), blk(b)] += dst[side, b, comp]

    for side in (0, 1):
        stage(grow_s.at[side], ga, 0 if side == 0 else TILE - WIDE, WIDE)
    send_rows(grow_s, grow_in, ("g",))
    backward(INNER, ga)

    def gcol_index(part):
        first, second = (WIDE, 2 * WIDE) if part == 0 else (0, TILE - WIDE)
        return [(first + j, second + j, j) for j in range(0, WIDE, MARGIN)]

    def gcol_pack(part):
        n = MARGIN
        lane = lane_iota(n)
        base = part * 288
        for row_a, row_b, j in gcol_index(part):
            for side in (0, 1):
                kept = []
                for row, at in ((row_a, j), (row_b, WIDE + j)):
                    re = ga[0, pl.ds(row, n), blk(0 if side == 0 else 2)]
                    im = ga[1, pl.ds(row, n), blk(0 if side == 0 else 2)]
                    if side == 1:
                        strip = jnp.where(lane < 96, pltpu.roll(re, 96, 1), pltpu.roll(im, 64, 1))
                    else:
                        strip = jnp.where(lane < 96, re, pltpu.roll(im, 96, 1))
                    gcol_s[side, pl.ds(base + at, n), :] = strip
                    kept.append(im)
                shift = (96, 32) if side == 0 else (64, 0)
                low = pltpu.roll(kept[0], shift[0], 1)
                high = pltpu.roll(kept[1], shift[1], 1) if shift[1] else kept[1]
                gcol_s[side, pl.ds(base + 192 + j, n), :] = jnp.where(lane < 64, low, high)

    def gcol_unpack(side, part):
        n = MARGIN
        lane = lane_iota(n)
        base = part * 288
        for row_a, row_b, j in gcol_index(part):
            rest = gcol_in[side, pl.ds(base + 192 + j, n), :]
            for row, at, shift in ((row_a, j, 0), (row_b, WIDE + j, 64)):
                strip = gcol_in[side, pl.ds(base + at, n), :]
                if side == 0:
                    re = jnp.where(lane < 96, strip, 0.0)
                    im = jnp.where(lane < 32, pltpu.roll(strip, 32, 1), pltpu.roll(rest, 32 + shift, 1))
                    im = jnp.where(lane < 96, im, 0.0)
                else:
                    re = jnp.where(lane < 32, 0.0, pltpu.roll(strip, 32, 1))
                    tail = pltpu.roll(rest, 64 + shift, 1) if shift == 0 else rest
                    im = jnp.where(lane < 64, pltpu.roll(strip, 64, 1), tail)
                    im = jnp.where(lane < 32, 0.0, im)
                b = 0 if side == 0 else 2
                ga[0, pl.ds(row, n), blk(b)] += re
                ga[1, pl.ds(row, n), blk(b)] += im

    def gcol_send(part):
        rows = pl.ds(part * 288, 288)
        for side in (0, 1):
            send(("col", side), 3 + part, gcol_s.at[side, rows, :], gcol_in.at[1 - side, rows, :])

    def gcol_add(part):
        rows = pl.ds(part * 288, 288)
        for side in (0, 1):
            arrived(("col", side), 3 + part, gcol_s.at[1 - side, rows, :], gcol_in.at[side, rows, :])

            @pl.when(has["col", side])
            def _(side=side):
                gcol_unpack(side, part)

    def update(rows):
        for at in rows:
            lane = lane_iota(MARGIN)
            ok = True
            if at == 0:
                ok = has["row", 0]
            elif at == TILE - MARGIN:
                ok = has["row", 1]
            keep = (
                jnp.logical_and(ok, jnp.logical_or(lane >= MARGIN, has["col", 0])),
                jnp.logical_and(ok, lane >= 0),
                jnp.logical_and(ok, jnp.logical_or(lane < 80, has["col", 1])),
            )
            for comp in (0, 1):
                for b in range(3):
                    cur[comp, pl.ds(at, MARGIN), blk(b)] += jnp.where(
                        keep[b], STEP * ga[comp, pl.ds(at, MARGIN), blk(b)], 0.0)

    gcol_pack(0)
    gcol_send(0)
    gcol_add(0)
    update(range(WIDE, TILE - WIDE, MARGIN))
    forward(INNER)

    first = (0, TILE - WIDE)
    add_rows(grow_s, grow_in, ("g",), ga, first, WIDE, (0, 2))
    gcol_pack(1)
    gcol_send(1)
    add_rows(grow_s, grow_in, ("g",), ga, first, WIDE, (1,))
    gcol_add(1)
    update((0, MARGIN, TILE - WIDE, TILE - MARGIN))

    edge_pass(gb)
    for side in (0, 1):
        stage(frow_s.at[side], gb, 0 if side == 0 else TILE - MARGIN, MARGIN)
    send_rows(frow_s, frow_in, ("f",))
    backward(INNER, gb)

    def fcol_rows(part):
        if part == 0:
            return 0, 48, [WIDE + 48 * k for k in range(4)]
        return 144, 24, [MARGIN, MARGIN + 24, TILE - WIDE, TILE - WIDE + 24]

    def fcol_pack(part):
        base, n, starts = fcol_rows(part)
        for side in (0, 1):
            pack(fcol_s.at[side], base, [
                pair_up(*(gb[comp, pl.ds(row, n), blk(2 * side)] for comp in (0, 1)), 80 * side) for row in starts])

    def fcol_send(part):
        base, n, _ = fcol_rows(part)
        for side in (0, 1):
            rows = pl.ds(base, 3 * n)
            send(("col", side), 5 + part, fcol_s.at[side, rows, :], fcol_in.at[1 - side, rows, :])

    def fcol_add(part):
        base, n, starts = fcol_rows(part)
        rows = pl.ds(base, 3 * n)
        for side in (0, 1):
            arrived(("col", side), 5 + part, fcol_s.at[1 - side, rows, :], fcol_in.at[side, rows, :])

            @pl.when(has["col", side])
            def _(side=side):
                first = MARGIN if side == 0 else 32
                lane = lane_iota(n)
                ok = jnp.logical_and(lane >= first, lane < first + MARGIN)
                for row, strip in zip(starts, unpack(fcol_in.at[side], base, n)):
                    for comp in (0, 1):
                        gb[comp, pl.ds(row, n), blk(2 * side)] += jnp.where(
                            ok, rolled(strip, first - MARGIN * comp), 0.0)

    def write(row):
        lane, rows, to_rows = lane_iota(MARGIN), pl.ds(row, MARGIN), pl.ds(row - MARGIN, MARGIN)
        for comp in (0, 1):
            v = [pltpu.roll(cur[comp, rows, blk(b)] + STEP * gb[comp, rows, blk(b)], 80, 1) for b in range(3)]
            out[comp, to_rows, blk(0)] = jnp.where(lane < 80, v[0], v[1])
            out[comp, to_rows, blk(1)] = jnp.where(lane < 80, v[1], v[2])
            out[comp, to_rows, pl.ds(256, 32)] = v[2][:, :32]

    fcol_pack(0)
    fcol_send(0)
    fcol_add(0)
    for row in range(WIDE, TILE - WIDE, MARGIN):
        write(row)
    first = (MARGIN, TILE - WIDE)
    add_rows(frow_s, frow_in, ("f",), gb, first, MARGIN, (0, 2))
    fcol_pack(1)
    fcol_send(1)
    add_rows(frow_s, frow_in, ("f",), gb, first, MARGIN, (1,))
    fcol_add(1)
    for row in first:
        write(row)

    for key, kind, src, dst in started:
        @pl.when(peer(key)[0])
        def _(args=(key, kind, src, dst, True)):
            remote(*args).wait_send()


def shards(object_field, probe, amplitudes, offsets, counts):
    tables = (jnp.asarray(a) for a in half_tables())
    anywhere = pl.BlockSpec(memory_space=pl.ANY)
    scalars = pl.BlockSpec(memory_space=pltpu.SMEM)
    v32 = lambda *shape: pltpu.VMEM(shape, F32)
    v16 = lambda *shape: pltpu.VMEM(shape, BF16)
    return pl.pallas_call(
        kernel,
        out_shape=jax.ShapeDtypeStruct(object_field.shape, F32),
        in_specs=[scalars, scalars] + [anywhere] * 7,
        out_specs=pl.BlockSpec(memory_space=pltpu.VMEM),
        scratch_shapes=[
            v32(2, CORE, CORE), v32(2, SIDE, SIDE), v16(1, 1, SLOTS, SIDE, SIDE),
            v16(SIDE, SIDE), v16(SIDE, SIDE), v16(SIDE, SIDE), v16(SIDE, SIDE),
            v32(SLOTS, 2, SIDE, SIDE), v32(SLOTS, SIDE, SIDE),
            v16(SLOTS, SIDE, 2 * SIDE), v16(2, SIDE, 2 * SIDE), v16(SLOTS, 2 * SIDE, SIDE), v16(2, SIDE, SIDE),
            v32(2, TILE, TILE), v32(2, TILE, TILE), v32(2, TILE, TILE),
            v32(2, 2, MARGIN, SIDE), v32(2, MARGIN // 2, HALF), v32(2, MARGIN // 2, HALF), v32(2, 3 * QUARTER, HALF), v32(2, 3 * QUARTER, HALF),
            v32(2, 2, MARGIN, HALF), v32(2, 2, MARGIN, HALF),
            v32(2, 3, 2, WIDE, HALF), v32(2, 3, 2, WIDE, HALF),
            v32(2, 576, HALF), v32(2, 576, HALF),
            v32(2, 3, 2, MARGIN, HALF), v32(2, 3, 2, MARGIN, HALF),
            v32(2, 216, HALF), v32(2, 216, HALF),
            pltpu.SemaphoreType.DMA((7,)),
            pltpu.SemaphoreType.DMA((30,)),
            pltpu.SemaphoreType.DMA((30,)),
        ],
        compiler_params=pltpu.CompilerParams(
            collective_id=0, has_side_effects=True, vmem_limit_bytes=60 * 1024 * 1024),
        name="ptycho",
    )(jnp.swapaxes(offsets, 2, 3), counts, object_field, probe, amplitudes, *tables)


def solution(mesh):
    return jax.shard_map(
        shards,
        mesh=mesh,
        in_specs=(
            P(None, "row", "col"),
            P(),
            P("row", "col", None, None, None),
            P("row", "col", None, None),
            P("row", "col"),
        ),
        out_specs=P(None, "row", "col"),
        check_vma=False,
    )
```

```python
import functools
import math

import jax
import jax.numpy as jnp
import numpy as np
from jax import lax
from jax.experimental import pallas as pl
from jax.experimental.pallas import tpu as pltpu
from jax.sharding import PartitionSpec as P

MARGIN = 48
PASSES = 2
SIDE = 256
HALF = 128
CORE = 288
TILE = 384
SLOTS = 8
STEP = 0.1
FLOOR = 0.01
F32 = jnp.float32
BF16 = jnp.bfloat16

WIDE = 2 * MARGIN
QUARTER = CORE // 4

EDGE, INNER = 0, HALF


def half_tables():
    position = np.arange(SIDE)
    angle = (position[:, None] * position[None, :] % SIDE) * (2.0 * math.pi / SIDE)
    scale = 1.0 / math.sqrt(SIDE)
    cosine, sine = np.cos(angle) * scale, np.sin(angle) * scale
    table = np.concatenate([cosine[:HALF], cosine[HALF : HALF + 1], sine[1:HALF]])
    order = np.concatenate([np.arange(HALF), [HALF], np.arange(SIDE - 1, HALF, -1)])
    swap = np.zeros((SIDE, SIDE), np.float32)
    swap[np.arange(SIDE), order] = 1.0
    paired = np.stack([table[:HALF].reshape(8, 16, SIDE), table[HALF:].reshape(8, 16, SIDE)], 1).reshape(SIDE, SIDE)
    return [a.astype(jnp.bfloat16) for a in (table, table.T, paired, swap)]


def mm(a, b):
    return jnp.dot(a, b, preferred_element_type=F32)


def lane_iota(rows):
    return lax.broadcasted_iota(jnp.int32, (rows, HALF), 1)


def row_iota(rows, start):
    return lax.broadcasted_iota(jnp.int32, (rows, HALF), 0) + start


def blk(n):
    return pl.ds(n * HALF, HALF)


def kernel(
    off, cnt, obj, probe, amp, table, table_t, paired, swap, out,
    ob, pb, ab, tv, ttv, tpv, sv,
    pr, ap, hb, wb, qb, xb, cur, ga, gb,
    row_in, tail_s, tail_in, col_s, col_in, corner_s, corner_in, grow_s, grow_in, gcol_s, gcol_in, frow_s, frow_in, fcol_s, fcol_in,
    load_sem, send_sem, recv_sem,
):
    n_row, n_col = lax.axis_size("row"), lax.axis_size("col")
    me_r, me_c = lax.axis_index("row"), lax.axis_index("col")
    has = {("row", 0): me_r > 0, ("row", 1): me_r < n_row - 1, ("col", 0): me_c > 0, ("col", 1): me_c < n_col - 1}
    to = {("row", 0): me_r - 1, ("row", 1): me_r + 1, ("col", 0): me_c - 1, ("col", 1): me_c + 1}
    sides = [(axis, side) for axis in ("row", "col") for side in (0, 1)]
    corners = [(a, b) for a in (0, 1) for b in (0, 1)]

    def peer(key):
        if key in has:
            return has[key], {key[0]: to[key]}
        rows, cols = ("row", key[0]), ("col", key[1])
        return jnp.logical_and(has[rows], has[cols]), {"row": to[rows], "col": to[cols]}

    def other(key):
        return (key[0], 1 - key[1]) if key in has else (1 - key[0], 1 - key[1])

    loads = [
        pltpu.make_async_copy(src, dst, load_sem.at[i])
        for i, (src, dst) in enumerate(
            ((obj, ob), (probe, pb), (amp, ab), (table, tv), (table_t, ttv), (paired, tpv), (swap, sv))
        )
    ]
    for copy in loads:
        copy.start()

    barrier = pltpu.get_barrier_semaphore()
    for key in sides + corners:
        ok, device = peer(key)

        @pl.when(ok)
        def _(device=device):
            pl.semaphore_signal(barrier, inc=1, device_id=device, device_id_type=pl.DeviceIdType.MESH)
    kinds, started = {}, []

    def semaphore(kind, key):
        return kinds.setdefault((kind, key), len(kinds))

    def remote(key, kind, src, dst, outgoing):
        here, there = (key, other(key)) if outgoing else (other(key), key)
        return pltpu.make_async_remote_copy(
            src_ref=src, dst_ref=dst,
            send_sem=send_sem.at[semaphore(kind, here)],
            recv_sem=recv_sem.at[semaphore(kind, there)],
            device_id=peer(key)[1],
            device_id_type=pl.DeviceIdType.MESH,
        )

    def send(key, kind, src, dst):
        started.append((key, kind, src, dst))

        @pl.when(peer(key)[0])
        def _():
            remote(key, kind, src, dst, True).start()

    def arrived(key, kind, src, dst):
        @pl.when(peer(key)[0])
        def _():
            remote(key, kind, src, dst, False).wait_recv()

    loads[0].wait()

    def own_rows(ref, comp, rows, n):
        tail = jnp.concatenate([ref[comp, rows, pl.ds(256, 32)], jnp.zeros((n, 96), F32)], 1)
        return ref[comp, rows, blk(0)], ref[comp, rows, blk(1)], tail

    def rolled(value, shift):
        return pltpu.roll(value, shift % HALF, 1) if shift % HALF else value

    def pack(dst, base, strips):
        n = strips[0].shape[0]
        lane = lane_iota(n)
        for k in range(3):
            dst[pl.ds(base + k * n, n), :] = jnp.where(lane < 96, strips[k], rolled(strips[3], 96 - 32 * k))

    def unpack(src, base, n):
        lane = lane_iota(n)
        three = [src[pl.ds(base + k * n, n), :] for k in range(3)]
        a, b, c = (rolled(v, 32 * k + 32) for k, v in enumerate(three))
        return three + [jnp.where(lane < 32, a, jnp.where(lane < 64, b, c))]

    def pair_up(re, im, at):
        return jnp.where(lane_iota(re.shape[0]) < MARGIN, rolled(re, -at), rolled(im, MARGIN - at))

    def own_strip(side, row, n):
        re, im = (own_rows(ob, comp, pl.ds(row, n), n) for comp in (0, 1))
        if side == 0:
            return pair_up(re[0], im[0], 0)
        lane = lane_iota(n)
        return pair_up(*(jnp.where(lane < 32, v[2], v[1]) for v in (re, im)), 112)

    def row_start(side):
        return 0 if side == 0 else CORE - MARGIN

    for side in (0, 1):
        part = [
            pltpu.roll(own_rows(ob, comp, pl.ds(row_start(side) + 24 * h, 24), 24)[2], 32 * (2 * h + comp), 1)
            if h + comp else own_rows(ob, comp, pl.ds(row_start(side), 24), 24)[2]
            for h in (0, 1) for comp in (0, 1)
        ]
        tail_s[side] = part[0] + part[1] + part[2] + part[3]

    for b in (0, 1):
        for a in (0, 1):
            corner_s[b, a] = own_strip(b, row_start(a), MARGIN)
        pack(col_s.at[b], 0, [own_strip(b, k * QUARTER, QUARTER) for k in range(4)])

    pl.semaphore_wait(barrier, sum(peer(key)[0].astype(jnp.int32) for key in sides + corners))

    for side in (0, 1):
        send(("col", side), 2, col_s.at[side], col_in.at[1 - side])
    for side in (0, 1):
        send(("row", side), 0, ob.at[:, pl.ds(row_start(side), MARGIN), pl.ds(0, SIDE)], row_in.at[1 - side])
        send(("row", side), 7, tail_s.at[side], tail_in.at[1 - side])
    for a, b in corners:
        send((a, b), 1, corner_s.at[b, a], corner_in.at[1 - b, 1 - a])

    def place(comp, rows, values):
        lane = lane_iota(values[0].shape[0])
        a, b, c = (pltpu.roll(v, MARGIN, 1) for v in values)
        cur[comp, rows, blk(0)] = jnp.where(lane < MARGIN, 0.0, a)
        cur[comp, rows, blk(1)] = jnp.where(lane < MARGIN, a, b)
        cur[comp, rows, blk(2)] = jnp.where(lane < MARGIN, b, c)

    @pl.loop(0, CORE // MARGIN)
    def _(i):
        at = pl.multiple_of(i * MARGIN, MARGIN)
        for comp in (0, 1):
            place(comp, pl.ds(MARGIN + at, MARGIN), own_rows(ob, comp, pl.ds(at, MARGIN), MARGIN))

    def place_columns(side, row, strip):
        n = strip.shape[0]
        lane, rows = lane_iota(n), pl.ds(row, n)
        for comp in (0, 1):
            if side == 0:
                new = rolled(strip, -MARGIN * comp)
                cur[comp, rows, blk(0)] = jnp.where(lane < MARGIN, new, cur[comp, rows, blk(0)])
            else:
                new = rolled(strip, 80 - MARGIN * comp)
                cur[comp, rows, blk(2)] = jnp.where(lane >= 80, new, cur[comp, rows, blk(2)])

    @pl.loop(0, TILE // MARGIN)
    def _(i):
        for ref in (ga, gb):
            for comp in (0, 1):
                ref[comp, pl.ds(pl.multiple_of(i * MARGIN, MARGIN), MARGIN), :] = jnp.zeros((MARGIN, TILE), F32)

    loads[1].wait()
    loads[2].wait()
    for copy in loads[3:]:
        copy.wait()
    live_count = cnt[0, 0]

    @pl.loop(0, SLOTS)
    def _(s):
        r, c = off[0, 0, 0, s], off[0, 0, 1, s]
        live = jnp.where(s < live_count, 1.0, 0.0).astype(F32)
        for comp in (0, 1):
            pr[s, comp] = pltpu.roll(pltpu.roll(pb[comp], r, 0), c, 1) * live
        ap[s] = mm(mm(sv[...], ab[0, 0, s]).astype(BF16), sv[...])

    def cols_fix(plain, other, lane):
        return jnp.where(lane == 0, other, plain)

    def forward_rows(s, first, buf):
        r, c = off[0, 0, 0, s], off[0, 0, 1, s]
        lane = lane_iota(16)
        hi_c = lane < c
        for at in range(0, HALF, 16):
            m = first + at
            patch = []
            for comp in (0, 1):
                if m < HALF:
                    hi_r = row_iota(16, m) < r
                    three = [
                        jnp.where(hi_r, cur[comp, pl.ds(m + SIDE, 16), blk(b)], cur[comp, pl.ds(m, 16), blk(b)])
                        for b in range(3)
                    ]
                else:
                    three = [cur[comp, pl.ds(m, 16), blk(b)] for b in range(3)]
                patch.append((jnp.where(hi_c, three[2], three[0]), three[1]))
            for b in (0, 1):
                p0, p1 = pr[s, 0, pl.ds(m, 16), blk(b)], pr[s, 1, pl.ds(m, 16), blk(b)]
                xb[buf, pl.ds(2 * at, 16), blk(b)] = (p0 * patch[0][b] - p1 * patch[1][b]).astype(BF16)
                xb[buf, pl.ds(2 * at + 16, 16), blk(b)] = (p0 * patch[1][b] + p1 * patch[0][b]).astype(BF16)
        v = mm(xb[buf], ttv[...])
        for at in range(0, HALF, 16):
            rows = pl.ds(first + at, 16)
            re, im = slice(2 * at, 2 * at + 16), slice(2 * at + 16, 2 * at + 32)
            c_r, s_r, c_i, s_i = v[re, :HALF], v[re, HALF:], v[im, :HALF], v[im, HALF:]
            hb[s, rows, blk(0)] = cols_fix(c_r + s_i, c_r, lane).astype(BF16)
            hb[s, rows, blk(1)] = cols_fix(c_r - s_i, s_r, lane).astype(BF16)
            hb[s, rows, blk(2)] = cols_fix(c_i - s_r, c_i, lane).astype(BF16)
            hb[s, rows, blk(3)] = cols_fix(c_i + s_r, s_i, lane).astype(BF16)

    def correct(s, buf, u):
        for k in range(0, HALF, 16):
            for b in (0, 1):
                lo, hi = slice(2 * k, 2 * k + 16), slice(2 * k + 16, 2 * k + 32)
                re, im = slice(b * HALF, b * HALF + HALF), slice(SIDE + b * HALF, SIDE + b * HALF + HALF)
                c_r, s_r, c_i, s_i = u[lo, re], u[hi, re], u[lo, im], u[hi, im]
                p_r, p_i, m_r, m_i = c_r + s_i, c_i - s_r, c_r - s_i, c_i + s_r
                if k == 0:
                    first = row_iota(16, 0) == 0
                    p_r, p_i = jnp.where(first, c_r, p_r), jnp.where(first, c_i, p_i)
                    m_r, m_i = jnp.where(first, s_r, m_r), jnp.where(first, s_i, m_i)
                f_p = ap[s, pl.ds(k, 16), blk(b)] * lax.rsqrt(p_r * p_r + p_i * p_i + FLOOR) - 1.0
                f_m = ap[s, pl.ds(HALF + k, 16), blk(b)] * lax.rsqrt(m_r * m_r + m_i * m_i + FLOOR) - 1.0
                p_r, p_i, m_r, m_i = p_r * f_p, p_i * f_p, m_r * f_m, m_i * f_m
                a_r, a_i, nb_i, b_r = p_r + m_r, p_i + m_i, m_i - p_i, p_r - m_r
                if k == 0:
                    a_r, a_i = jnp.where(first, p_r, a_r), jnp.where(first, p_i, a_i)
                    nb_i, b_r = jnp.where(first, m_r, nb_i), jnp.where(first, m_i, b_r)
                wb[buf, pl.ds(k, 16), blk(b)] = a_r.astype(BF16)
                wb[buf, pl.ds(k, 16), blk(2 + b)] = a_i.astype(BF16)
                wb[buf, pl.ds(HALF + k, 16), blk(b)] = nb_i.astype(BF16)
                wb[buf, pl.ds(HALF + k, 16), blk(2 + b)] = b_r.astype(BF16)

    def split_columns(s, y):
        lane = lane_iota(16)
        for m in range(0, SIDE, 16):
            rows = slice(m, m + 16)
            p_r, m_r, p_i, m_i = (y[rows, b * HALF : b * HALF + HALF] for b in range(4))
            re, im = 2 * m, 2 * m + 16
            qb[s, pl.ds(re, 16), blk(0)] = cols_fix(p_r + m_r, p_r, lane).astype(BF16)
            qb[s, pl.ds(re, 16), blk(1)] = cols_fix(m_i - p_i, m_r, lane).astype(BF16)
            qb[s, pl.ds(im, 16), blk(0)] = cols_fix(p_i + m_i, p_i, lane).astype(BF16)
            qb[s, pl.ds(im, 16), blk(1)] = cols_fix(p_r - m_r, m_i, lane).astype(BF16)

    def backward_rows(s, first, g):
        products = [mm(qb[slot, pl.ds(2 * first, SIDE), :], tv[...]) for slot in s]
        lane = lane_iota(16)
        for at in range(0, HALF, 16):
            m = first + at
            total = [[None] * 3, [None] * 3]
            below = [[None] * 3, [None] * 3]
            for slot, v in zip(s, products):
                r, c = off[0, 0, 0, slot], off[0, 0, 1, slot]
                terms = ([], [])
                for b in (0, 1):
                    b_r = v[2 * at : 2 * at + 16, b * HALF : b * HALF + HALF]
                    b_i = v[2 * at + 16 : 2 * at + 32, b * HALF : b * HALF + HALF]
                    p0, p1 = pr[slot, 0, pl.ds(m, 16), blk(b)], pr[slot, 1, pl.ds(m, 16), blk(b)]
                    terms[0].append(p0 * b_r + p1 * b_i)
                    terms[1].append(p0 * b_i - p1 * b_r)
                for comp in (0, 1):
                    left = terms[comp][0]
                    high = jnp.where(lane < c, left, 0.0)
                    for b, value in enumerate((left - high, terms[comp][1], high)):
                        if m < HALF:
                            low = jnp.where(row_iota(16, m) < r, value, 0.0)
                            value = value - low
                            below[comp][b] = low if below[comp][b] is None else below[comp][b] + low
                        total[comp][b] = value if total[comp][b] is None else total[comp][b] + value
            for comp in (0, 1):
                for b in range(3):
                    g[comp, pl.ds(m, 16), blk(b)] += total[comp][b]
                    if m < HALF:
                        g[comp, pl.ds(m + SIDE, 16), blk(b)] += below[comp][b]

    def forward(first):
        @pl.loop(0, SLOTS // 2)
        def _(i):
            for buf in (0, 1):
                forward_rows(2 * i + buf, first, buf)

    def edge_pass(g):
        @pl.loop(0, SLOTS // 2)
        def _(i):
            pair = (2 * i, 2 * i + 1)
            for buf in (0, 1):
                forward_rows(pair[buf], EDGE, buf)
            far = [mm(tpv[...], hb[s]) for s in pair]
            back = []
            for buf in (0, 1):
                correct(pair[buf], buf, far[buf])
                back.append(mm(ttv[...], wb[buf]))
            for buf in (0, 1):
                split_columns(pair[buf], back[buf])
            backward_rows(pair, EDGE, g)

    def backward(first, g):
        @pl.loop(0, SLOTS // 2)
        def _(i):
            backward_rows((2 * i, 2 * i + 1), first, g)

    for side in (0, 1):
        arrived(("col", side), 2, col_s.at[1 - side], col_in.at[side])

        @pl.when(has["col", side])
        def _(side=side):
            for k, strip in enumerate(unpack(col_in.at[side], 0, QUARTER)):
                place_columns(side, MARGIN + k * QUARTER, strip)

    forward(INNER)

    for side in (0, 1):
        first = 0 if side == 0 else TILE - MARGIN
        arrived(("row", side), 0, ob.at[:, pl.ds(0, MARGIN), pl.ds(0, SIDE)], row_in.at[side])
        arrived(("row", side), 7, tail_s.at[1 - side], tail_in.at[side])

        @pl.when(has["row", side])
        def _(side=side, first=first):
            lane = lane_iota(24)
            for h in (0, 1):
                for comp in (0, 1):
                    shift = (HALF - 32 * (2 * h + comp)) % HALF
                    tail = tail_in[side] if shift == 0 else pltpu.roll(tail_in[side], shift, 1)
                    rows = pl.ds(24 * h, 24)
                    place(comp, pl.ds(first + 24 * h, 24),
                          (row_in[side, comp, rows, blk(0)], row_in[side, comp, rows, blk(1)],
                           jnp.where(lane < 32, tail, 0.0)))

        @pl.when(jnp.logical_not(has["row", side]))
        def _(first=first):
            for comp in (0, 1):
                cur[comp, pl.ds(first, MARGIN), :] = jnp.zeros((MARGIN, TILE), F32)
    for a, b in corners:
        arrived((a, b), 1, corner_s.at[1 - b, 1 - a], corner_in.at[b, a])

        @pl.when(peer((a, b))[0])
        def _(a=a, b=b):
            place_columns(b, a * (TILE - MARGIN), corner_in[b, a])

    edge_pass(ga)

    def stage(dst, g, src_row, n_rows):
        for b in range(3):
            for comp in (0, 1):
                dst[b, comp] = g[comp, pl.ds(src_row, n_rows), blk(b)]

    def send_rows(src, dst, kind, blocks):
        for side in (0, 1):
            for b in blocks:
                send(("row", side), kind + (b,), src.at[side, b], dst.at[1 - side, b])

    def add_rows(src, dst, kind, g, first, n_rows, blocks):
        for side in (0, 1):
            for b in blocks:
                arrived(("row", side), kind + (b,), src.at[1 - side, b], dst.at[side, b])

            @pl.when(has["row", side])
            def _(side=side):
                for b in blocks:
                    for comp in (0, 1):
                        g[comp, pl.ds(first[side], n_rows), blk(b)] += dst[side, b, comp]

    for side in (0, 1):
        stage(grow_s.at[side], ga, 0 if side == 0 else TILE - WIDE, WIDE)
    send_rows(grow_s, grow_in, ("g",), (0, 2))
    backward(INNER, ga)

    def gcol_index(part):
        first, second = (WIDE, 2 * WIDE) if part == 0 else (0, TILE - WIDE)
        return [(first + j, second + j, j) for j in range(0, WIDE, MARGIN)]

    def gcol_pack(part):
        n = MARGIN
        lane = lane_iota(n)
        base = part * 288
        for row_a, row_b, j in gcol_index(part):
            for side in (0, 1):
                kept = []
                for row, at in ((row_a, j), (row_b, WIDE + j)):
                    re = ga[0, pl.ds(row, n), blk(0 if side == 0 else 2)]
                    im = ga[1, pl.ds(row, n), blk(0 if side == 0 else 2)]
                    if side == 1:
                        strip = jnp.where(lane < 96, pltpu.roll(re, 96, 1), pltpu.roll(im, 64, 1))
                    else:
                        strip = jnp.where(lane < 96, re, pltpu.roll(im, 96, 1))
                    gcol_s[side, pl.ds(base + at, n), :] = strip
                    kept.append(im)
                shift = (96, 32) if side == 0 else (64, 0)
                low = pltpu.roll(kept[0], shift[0], 1)
                high = pltpu.roll(kept[1], shift[1], 1) if shift[1] else kept[1]
                gcol_s[side, pl.ds(base + 192 + j, n), :] = jnp.where(lane < 64, low, high)

    def gcol_unpack(side, part):
        n = MARGIN
        lane = lane_iota(n)
        base = part * 288
        for row_a, row_b, j in gcol_index(part):
            rest = gcol_in[side, pl.ds(base + 192 + j, n), :]
            for row, at, shift in ((row_a, j, 0), (row_b, WIDE + j, 64)):
                strip = gcol_in[side, pl.ds(base + at, n), :]
                if side == 0:
                    re = jnp.where(lane < 96, strip, 0.0)
                    im = jnp.where(lane < 32, pltpu.roll(strip, 32, 1), pltpu.roll(rest, 32 + shift, 1))
                    im = jnp.where(lane < 96, im, 0.0)
                else:
                    re = jnp.where(lane < 32, 0.0, pltpu.roll(strip, 32, 1))
                    tail = pltpu.roll(rest, 64 + shift, 1) if shift == 0 else rest
                    im = jnp.where(lane < 64, pltpu.roll(strip, 64, 1), tail)
                    im = jnp.where(lane < 32, 0.0, im)
                b = 0 if side == 0 else 2
                ga[0, pl.ds(row, n), blk(b)] += re
                ga[1, pl.ds(row, n), blk(b)] += im

    def gcol_send(part):
        rows = pl.ds(part * 288, 288)
        for side in (0, 1):
            send(("col", side), 3 + part, gcol_s.at[side, rows, :], gcol_in.at[1 - side, rows, :])

    def gcol_add(part):
        rows = pl.ds(part * 288, 288)
        for side in (0, 1):
            arrived(("col", side), 3 + part, gcol_s.at[1 - side, rows, :], gcol_in.at[side, rows, :])

            @pl.when(has["col", side])
            def _(side=side):
                gcol_unpack(side, part)

    def update(rows):
        for at in rows:
            lane = lane_iota(MARGIN)
            ok = True
            if at == 0:
                ok = has["row", 0]
            elif at == TILE - MARGIN:
                ok = has["row", 1]
            keep = (
                jnp.logical_and(ok, jnp.logical_or(lane >= MARGIN, has["col", 0])),
                jnp.logical_and(ok, lane >= 0),
                jnp.logical_and(ok, jnp.logical_or(lane < 80, has["col", 1])),
            )
            for comp in (0, 1):
                for b in range(3):
                    cur[comp, pl.ds(at, MARGIN), blk(b)] += jnp.where(
                        keep[b], STEP * ga[comp, pl.ds(at, MARGIN), blk(b)], 0.0)

    gcol_pack(0)
    gcol_send(0)
    first = (0, TILE - WIDE)
    add_rows(grow_s, grow_in, ("g",), ga, first, WIDE, (0, 2))
    gcol_pack(1)
    gcol_send(1)
    send_rows(grow_s, grow_in, ("g",), (1,))
    gcol_add(0)
    update(range(WIDE, TILE - WIDE, MARGIN))
    forward(INNER)
    gcol_add(1)
    add_rows(grow_s, grow_in, ("g",), ga, first, WIDE, (1,))
    update((0, MARGIN, TILE - WIDE, TILE - MARGIN))

    edge_pass(gb)
    for side in (0, 1):
        stage(frow_s.at[side], gb, 0 if side == 0 else TILE - MARGIN, MARGIN)
    send_rows(frow_s, frow_in, ("f",), (0, 2))
    backward(INNER, gb)

    def fcol_rows(part):
        if part == 0:
            return 0, 48, [WIDE + 48 * k for k in range(4)]
        return 144, 24, [MARGIN, MARGIN + 24, TILE - WIDE, TILE - WIDE + 24]

    def fcol_pack(part):
        base, n, starts = fcol_rows(part)
        for side in (0, 1):
            pack(fcol_s.at[side], base, [
                pair_up(*(gb[comp, pl.ds(row, n), blk(2 * side)] for comp in (0, 1)), 80 * side) for row in starts])

    def fcol_send(part):
        base, n, _ = fcol_rows(part)
        for side in (0, 1):
            rows = pl.ds(base, 3 * n)
            send(("col", side), 5 + part, fcol_s.at[side, rows, :], fcol_in.at[1 - side, rows, :])

    def fcol_add(part):
        base, n, starts = fcol_rows(part)
        rows = pl.ds(base, 3 * n)
        for side in (0, 1):
            arrived(("col", side), 5 + part, fcol_s.at[1 - side, rows, :], fcol_in.at[side, rows, :])

            @pl.when(has["col", side])
            def _(side=side):
                first = MARGIN if side == 0 else 32
                lane = lane_iota(n)
                ok = jnp.logical_and(lane >= first, lane < first + MARGIN)
                for row, strip in zip(starts, unpack(fcol_in.at[side], base, n)):
                    for comp in (0, 1):
                        gb[comp, pl.ds(row, n), blk(2 * side)] += jnp.where(
                            ok, rolled(strip, first - MARGIN * comp), 0.0)

    def write(row):
        lane, rows, to_rows = lane_iota(MARGIN), pl.ds(row, MARGIN), pl.ds(row - MARGIN, MARGIN)
        for comp in (0, 1):
            v = [pltpu.roll(cur[comp, rows, blk(b)] + STEP * gb[comp, rows, blk(b)], 80, 1) for b in range(3)]
            out[comp, to_rows, blk(0)] = jnp.where(lane < 80, v[0], v[1])
            out[comp, to_rows, blk(1)] = jnp.where(lane < 80, v[1], v[2])
            out[comp, to_rows, pl.ds(256, 32)] = v[2][:, :32]

    fcol_pack(0)
    fcol_send(0)
    send_rows(frow_s, frow_in, ("f",), (1,))
    first = (MARGIN, TILE - WIDE)
    add_rows(frow_s, frow_in, ("f",), gb, first, MARGIN, (0, 2))
    fcol_pack(1)
    fcol_send(1)
    fcol_add(0)
    for row in range(WIDE, TILE - WIDE, MARGIN):
        write(row)
    add_rows(frow_s, frow_in, ("f",), gb, first, MARGIN, (1,))
    fcol_add(1)
    for row in first:
        write(row)

    for key, kind, src, dst in started:
        @pl.when(peer(key)[0])
        def _(args=(key, kind, src, dst, True)):
            remote(*args).wait_send()


def shards(object_field, probe, amplitudes, offsets, counts):
    tables = (jnp.asarray(a) for a in half_tables())
    anywhere = pl.BlockSpec(memory_space=pl.ANY)
    scalars = pl.BlockSpec(memory_space=pltpu.SMEM)
    v32 = lambda *shape: pltpu.VMEM(shape, F32)
    v16 = lambda *shape: pltpu.VMEM(shape, BF16)
    return pl.pallas_call(
        kernel,
        out_shape=jax.ShapeDtypeStruct(object_field.shape, F32),
        in_specs=[scalars, scalars] + [anywhere] * 7,
        out_specs=pl.BlockSpec(memory_space=pltpu.VMEM),
        scratch_shapes=[
            v32(2, CORE, CORE), v32(2, SIDE, SIDE), v16(1, 1, SLOTS, SIDE, SIDE),
            v16(SIDE, SIDE), v16(SIDE, SIDE), v16(SIDE, SIDE), v16(SIDE, SIDE),
            v32(SLOTS, 2, SIDE, SIDE), v32(SLOTS, SIDE, SIDE),
            v16(SLOTS, SIDE, 2 * SIDE), v16(2, SIDE, 2 * SIDE), v16(SLOTS, 2 * SIDE, SIDE), v16(2, SIDE, SIDE),
            v32(2, TILE, TILE), v32(2, TILE, TILE), v32(2, TILE, TILE),
            v32(2, 2, MARGIN, SIDE), v32(2, MARGIN // 2, HALF), v32(2, MARGIN // 2, HALF), v32(2, 3 * QUARTER, HALF), v32(2, 3 * QUARTER, HALF),
            v32(2, 2, MARGIN, HALF), v32(2, 2, MARGIN, HALF),
            v32(2, 3, 2, WIDE, HALF), v32(2, 3, 2, WIDE, HALF),
            v32(2, 576, HALF), v32(2, 576, HALF),
            v32(2, 3, 2, MARGIN, HALF), v32(2, 3, 2, MARGIN, HALF),
            v32(2, 216, HALF), v32(2, 216, HALF),
            pltpu.SemaphoreType.DMA((7,)),
            pltpu.SemaphoreType.DMA((30,)),
            pltpu.SemaphoreType.DMA((30,)),
        ],
        compiler_params=pltpu.CompilerParams(
            collective_id=0, has_side_effects=True, vmem_limit_bytes=60 * 1024 * 1024),
        name="ptycho",
    )(jnp.swapaxes(offsets, 2, 3), counts, object_field, probe, amplitudes, *tables)


def solution(mesh):
    return jax.shard_map(
        shards,
        mesh=mesh,
        in_specs=(
            P(None, "row", "col"),
            P(),
            P("row", "col", None, None, None),
            P("row", "col", None, None),
            P("row", "col"),
        ),
        out_specs=P(None, "row", "col"),
        check_vma=False,
    )
```

```python
import functools
import math

import jax
import jax.numpy as jnp
import numpy as np
from jax import lax
from jax.experimental import pallas as pl
from jax.experimental.pallas import tpu as pltpu
from jax.sharding import PartitionSpec as P

MARGIN = 48
PASSES = 2
SIDE = 256
HALF = 128
CORE = 288
TILE = 384
SLOTS = 8
STEP = 0.1
FLOOR = 0.01
F32 = jnp.float32
BF16 = jnp.bfloat16

WIDE = 2 * MARGIN
QUARTER = CORE // 4

EDGE, INNER = 0, HALF


def half_tables():
    position = np.arange(SIDE)
    angle = (position[:, None] * position[None, :] % SIDE) * (2.0 * math.pi / SIDE)
    scale = 1.0 / math.sqrt(SIDE)
    cosine, sine = np.cos(angle) * scale, np.sin(angle) * scale
    table = np.concatenate([cosine[:HALF], cosine[HALF : HALF + 1], sine[1:HALF]])
    order = np.concatenate([np.arange(HALF), [HALF], np.arange(SIDE - 1, HALF, -1)])
    swap = np.zeros((SIDE, SIDE), np.float32)
    swap[np.arange(SIDE), order] = 1.0
    paired = np.stack([table[:HALF].reshape(8, 16, SIDE), table[HALF:].reshape(8, 16, SIDE)], 1).reshape(SIDE, SIDE)
    return [a.astype(jnp.bfloat16) for a in (table, table.T, paired, swap)]


def mm(a, b):
    return jnp.dot(a, b, preferred_element_type=F32)


def lane_iota(rows):
    return lax.broadcasted_iota(jnp.int32, (rows, HALF), 1)


def row_iota(rows, start):
    return lax.broadcasted_iota(jnp.int32, (rows, HALF), 0) + start


def blk(n):
    return pl.ds(n * HALF, HALF)


def kernel(
    off, cnt, obj, probe, amp, table, table_t, paired, swap, out,
    ob, pb, ab, tv, ttv, tpv, sv,
    pr, ap, hb, wb, qb, xb, cur, ga, gb,
    row_in, tail_s, tail_in, col_s, col_in, corner_s, corner_in, grow_s, grow_in, gcol_s, gcol_in, frow_s, frow_in, fcol_s, fcol_in,
    load_sem, send_sem, recv_sem,
):
    n_row, n_col = lax.axis_size("row"), lax.axis_size("col")
    me_r, me_c = lax.axis_index("row"), lax.axis_index("col")
    has = {("row", 0): me_r > 0, ("row", 1): me_r < n_row - 1, ("col", 0): me_c > 0, ("col", 1): me_c < n_col - 1}
    to = {("row", 0): me_r - 1, ("row", 1): me_r + 1, ("col", 0): me_c - 1, ("col", 1): me_c + 1}
    sides = [(axis, side) for axis in ("row", "col") for side in (0, 1)]
    corners = [(a, b) for a in (0, 1) for b in (0, 1)]

    def peer(key):
        if key in has:
            return has[key], {key[0]: to[key]}
        rows, cols = ("row", key[0]), ("col", key[1])
        return jnp.logical_and(has[rows], has[cols]), {"row": to[rows], "col": to[cols]}

    def other(key):
        return (key[0], 1 - key[1]) if key in has else (1 - key[0], 1 - key[1])

    loads = [
        pltpu.make_async_copy(src, dst, load_sem.at[i])
        for i, (src, dst) in enumerate(
            ((obj, ob), (probe, pb), (amp, ab), (table, tv), (table_t, ttv), (paired, tpv), (swap, sv))
        )
    ]
    for copy in loads:
        copy.start()

    barrier = pltpu.get_barrier_semaphore()
    for key in sides + corners:
        ok, device = peer(key)

        @pl.when(ok)
        def _(device=device):
            pl.semaphore_signal(barrier, inc=1, device_id=device, device_id_type=pl.DeviceIdType.MESH)
    kinds, started = {}, []

    def semaphore(kind, key):
        return kinds.setdefault((kind, key), len(kinds))

    def remote(key, kind, src, dst, outgoing):
        here, there = (key, other(key)) if outgoing else (other(key), key)
        return pltpu.make_async_remote_copy(
            src_ref=src, dst_ref=dst,
            send_sem=send_sem.at[semaphore(kind, here)],
            recv_sem=recv_sem.at[semaphore(kind, there)],
            device_id=peer(key)[1],
            device_id_type=pl.DeviceIdType.MESH,
        )

    def send(key, kind, src, dst):
        started.append((key, kind, src, dst))

        @pl.when(peer(key)[0])
        def _():
            remote(key, kind, src, dst, True).start()

    def arrived(key, kind, src, dst):
        @pl.when(peer(key)[0])
        def _():
            remote(key, kind, src, dst, False).wait_recv()

    loads[0].wait()

    def own_rows(ref, comp, rows, n):
        tail = jnp.concatenate([ref[comp, rows, pl.ds(256, 32)], jnp.zeros((n, 96), F32)], 1)
        return ref[comp, rows, blk(0)], ref[comp, rows, blk(1)], tail

    def rolled(value, shift):
        return pltpu.roll(value, shift % HALF, 1) if shift % HALF else value

    def pack(dst, base, strips):
        n = strips[0].shape[0]
        lane = lane_iota(n)
        for k in range(3):
            dst[pl.ds(base + k * n, n), :] = jnp.where(lane < 96, strips[k], rolled(strips[3], 96 - 32 * k))

    def unpack(src, base, n):
        lane = lane_iota(n)
        three = [src[pl.ds(base + k * n, n), :] for k in range(3)]
        a, b, c = (rolled(v, 32 * k + 32) for k, v in enumerate(three))
        return three + [jnp.where(lane < 32, a, jnp.where(lane < 64, b, c))]

    def pair_up(re, im, at):
        return jnp.where(lane_iota(re.shape[0]) < MARGIN, rolled(re, -at), rolled(im, MARGIN - at))

    def own_strip(side, row, n):
        re, im = (own_rows(ob, comp, pl.ds(row, n), n) for comp in (0, 1))
        if side == 0:
            return pair_up(re[0], im[0], 0)
        lane = lane_iota(n)
        return pair_up(*(jnp.where(lane < 32, v[2], v[1]) for v in (re, im)), 112)

    def row_start(side):
        return 0 if side == 0 else CORE - MARGIN

    for side in (0, 1):
        part = [
            pltpu.roll(own_rows(ob, comp, pl.ds(row_start(side) + 24 * h, 24), 24)[2], 32 * (2 * h + comp), 1)
            if h + comp else own_rows(ob, comp, pl.ds(row_start(side), 24), 24)[2]
            for h in (0, 1) for comp in (0, 1)
        ]
        tail_s[side] = part[0] + part[1] + part[2] + part[3]

    for b in (0, 1):
        for a in (0, 1):
            corner_s[b, a] = own_strip(b, row_start(a), MARGIN)
        pack(col_s.at[b], 0, [own_strip(b, k * QUARTER, QUARTER) for k in range(4)])

    pl.semaphore_wait(barrier, sum(peer(key)[0].astype(jnp.int32) for key in sides + corners))

    for side in (0, 1):
        send(("col", side), 2, col_s.at[side], col_in.at[1 - side])
    for side in (0, 1):
        send(("row", side), 0, ob.at[:, pl.ds(row_start(side), MARGIN), pl.ds(0, SIDE)], row_in.at[1 - side])
        send(("row", side), 7, tail_s.at[side], tail_in.at[1 - side])
    for a, b in corners:
        send((a, b), 1, corner_s.at[b, a], corner_in.at[1 - b, 1 - a])

    def place(comp, rows, values):
        lane = lane_iota(values[0].shape[0])
        a, b, c = (pltpu.roll(v, MARGIN, 1) for v in values)
        cur[comp, rows, blk(0)] = jnp.where(lane < MARGIN, 0.0, a)
        cur[comp, rows, blk(1)] = jnp.where(lane < MARGIN, a, b)
        cur[comp, rows, blk(2)] = jnp.where(lane < MARGIN, b, c)

    @pl.loop(0, CORE // MARGIN)
    def _(i):
        at = pl.multiple_of(i * MARGIN, MARGIN)
        for comp in (0, 1):
            place(comp, pl.ds(MARGIN + at, MARGIN), own_rows(ob, comp, pl.ds(at, MARGIN), MARGIN))

    def place_columns(side, row, strip):
        n = strip.shape[0]
        lane, rows = lane_iota(n), pl.ds(row, n)
        for comp in (0, 1):
            if side == 0:
                new = rolled(strip, -MARGIN * comp)
                cur[comp, rows, blk(0)] = jnp.where(lane < MARGIN, new, cur[comp, rows, blk(0)])
            else:
                new = rolled(strip, 80 - MARGIN * comp)
                cur[comp, rows, blk(2)] = jnp.where(lane >= 80, new, cur[comp, rows, blk(2)])

    @pl.loop(0, TILE // MARGIN)
    def _(i):
        for ref in (ga, gb):
            for comp in (0, 1):
                ref[comp, pl.ds(pl.multiple_of(i * MARGIN, MARGIN), MARGIN), :] = jnp.zeros((MARGIN, TILE), F32)

    loads[1].wait()
    loads[2].wait()
    for copy in loads[3:]:
        copy.wait()
    live_count = cnt[0, 0]

    @pl.loop(0, SLOTS)
    def _(s):
        r, c = off[0, 0, 0, s], off[0, 0, 1, s]
        live = jnp.where(s < live_count, 1.0, 0.0).astype(F32)
        for comp in (0, 1):
            pr[s, comp] = pltpu.roll(pltpu.roll(pb[comp], r, 0), c, 1) * live
        ap[s] = mm(mm(sv[...], ab[0, 0, s]).astype(BF16), sv[...])

    def cols_fix(plain, other, lane):
        return jnp.where(lane == 0, other, plain)

    def forward_rows(s, first, buf):
        r, c = off[0, 0, 0, s], off[0, 0, 1, s]
        lane = lane_iota(16)
        hi_c = lane < c
        for at in range(0, HALF, 16):
            m = first + at
            patch = []
            for comp in (0, 1):
                if m < HALF:
                    hi_r = row_iota(16, m) < r
                    three = [
                        jnp.where(hi_r, cur[comp, pl.ds(m + SIDE, 16), blk(b)], cur[comp, pl.ds(m, 16), blk(b)])
                        for b in range(3)
                    ]
                else:
                    three = [cur[comp, pl.ds(m, 16), blk(b)] for b in range(3)]
                patch.append((jnp.where(hi_c, three[2], three[0]), three[1]))
            for b in (0, 1):
                p0, p1 = pr[s, 0, pl.ds(m, 16), blk(b)], pr[s, 1, pl.ds(m, 16), blk(b)]
                xb[buf, pl.ds(2 * at, 16), blk(b)] = (p0 * patch[0][b] - p1 * patch[1][b]).astype(BF16)
                xb[buf, pl.ds(2 * at + 16, 16), blk(b)] = (p0 * patch[1][b] + p1 * patch[0][b]).astype(BF16)
        v = mm(xb[buf], ttv[...])
        for at in range(0, HALF, 16):
            rows = pl.ds(first + at, 16)
            re, im = slice(2 * at, 2 * at + 16), slice(2 * at + 16, 2 * at + 32)
            c_r, s_r, c_i, s_i = v[re, :HALF], v[re, HALF:], v[im, :HALF], v[im, HALF:]
            hb[s, rows, blk(0)] = cols_fix(c_r + s_i, c_r, lane).astype(BF16)
            hb[s, rows, blk(1)] = cols_fix(c_r - s_i, s_r, lane).astype(BF16)
            hb[s, rows, blk(2)] = cols_fix(c_i - s_r, c_i, lane).astype(BF16)
            hb[s, rows, blk(3)] = cols_fix(c_i + s_r, s_i, lane).astype(BF16)

    def correct(s, buf, u):
        for k in range(0, HALF, 16):
            for b in (0, 1):
                lo, hi = slice(2 * k, 2 * k + 16), slice(2 * k + 16, 2 * k + 32)
                re, im = slice(b * HALF, b * HALF + HALF), slice(SIDE + b * HALF, SIDE + b * HALF + HALF)
                c_r, s_r, c_i, s_i = u[lo, re], u[hi, re], u[lo, im], u[hi, im]
                p_r, p_i, m_r, m_i = c_r + s_i, c_i - s_r, c_r - s_i, c_i + s_r
                if k == 0:
                    first = row_iota(16, 0) == 0
                    p_r, p_i = jnp.where(first, c_r, p_r), jnp.where(first, c_i, p_i)
                    m_r, m_i = jnp.where(first, s_r, m_r), jnp.where(first, s_i, m_i)
                f_p = ap[s, pl.ds(k, 16), blk(b)] * lax.rsqrt(p_r * p_r + p_i * p_i + FLOOR) - 1.0
                f_m = ap[s, pl.ds(HALF + k, 16), blk(b)] * lax.rsqrt(m_r * m_r + m_i * m_i + FLOOR) - 1.0
                p_r, p_i, m_r, m_i = p_r * f_p, p_i * f_p, m_r * f_m, m_i * f_m
                a_r, a_i, nb_i, b_r = p_r + m_r, p_i + m_i, m_i - p_i, p_r - m_r
                if k == 0:
                    a_r, a_i = jnp.where(first, p_r, a_r), jnp.where(first, p_i, a_i)
                    nb_i, b_r = jnp.where(first, m_r, nb_i), jnp.where(first, m_i, b_r)
                wb[buf, pl.ds(k, 16), blk(b)] = a_r.astype(BF16)
                wb[buf, pl.ds(k, 16), blk(2 + b)] = a_i.astype(BF16)
                wb[buf, pl.ds(HALF + k, 16), blk(b)] = nb_i.astype(BF16)
                wb[buf, pl.ds(HALF + k, 16), blk(2 + b)] = b_r.astype(BF16)

    def split_columns(s, y):
        lane = lane_iota(16)
        for m in range(0, SIDE, 16):
            rows = slice(m, m + 16)
            p_r, m_r, p_i, m_i = (y[rows, b * HALF : b * HALF + HALF] for b in range(4))
            re, im = 2 * m, 2 * m + 16
            qb[s, pl.ds(re, 16), blk(0)] = cols_fix(p_r + m_r, p_r, lane).astype(BF16)
            qb[s, pl.ds(re, 16), blk(1)] = cols_fix(m_i - p_i, m_r, lane).astype(BF16)
            qb[s, pl.ds(im, 16), blk(0)] = cols_fix(p_i + m_i, p_i, lane).astype(BF16)
            qb[s, pl.ds(im, 16), blk(1)] = cols_fix(p_r - m_r, m_i, lane).astype(BF16)

    def backward_rows(s, first, g):
        products = [mm(qb[slot, pl.ds(2 * first, SIDE), :], tv[...]) for slot in s]
        lane = lane_iota(16)
        for at in range(0, HALF, 16):
            m = first + at
            total = [[None] * 3, [None] * 3]
            below = [[None] * 3, [None] * 3]
            for slot, v in zip(s, products):
                r, c = off[0, 0, 0, slot], off[0, 0, 1, slot]
                terms = ([], [])
                for b in (0, 1):
                    b_r = v[2 * at : 2 * at + 16, b * HALF : b * HALF + HALF]
                    b_i = v[2 * at + 16 : 2 * at + 32, b * HALF : b * HALF + HALF]
                    p0, p1 = pr[slot, 0, pl.ds(m, 16), blk(b)], pr[slot, 1, pl.ds(m, 16), blk(b)]
                    terms[0].append(p0 * b_r + p1 * b_i)
                    terms[1].append(p0 * b_i - p1 * b_r)
                for comp in (0, 1):
                    left = terms[comp][0]
                    high = jnp.where(lane < c, left, 0.0)
                    for b, value in enumerate((left - high, terms[comp][1], high)):
                        if m < HALF:
                            low = jnp.where(row_iota(16, m) < r, value, 0.0)
                            value = value - low
                            below[comp][b] = low if below[comp][b] is None else below[comp][b] + low
                        total[comp][b] = value if total[comp][b] is None else total[comp][b] + value
            for comp in (0, 1):
                for b in range(3):
                    g[comp, pl.ds(m, 16), blk(b)] += total[comp][b]
                    if m < HALF:
                        g[comp, pl.ds(m + SIDE, 16), blk(b)] += below[comp][b]

    def forward(first):
        @pl.loop(0, SLOTS // 2)
        def _(i):
            for buf in (0, 1):
                forward_rows(2 * i + buf, first, buf)

    def edge_pass(g):
        def pair(i):
            return 2 * i, 2 * i + 1

        def first(i):
            for buf in (0, 1):
                forward_rows(pair(i)[buf], EDGE, buf)

        def middle(i, before, after):
            far = [mm(tpv[...], hb[s]) for s in pair(i)]
            before()
            back = []
            for buf in (0, 1):
                correct(pair(i)[buf], buf, far[buf])
                back.append(mm(ttv[...], wb[buf]))
            after()
            for buf in (0, 1):
                split_columns(pair(i)[buf], back[buf])

        def last(i):
            backward_rows(pair(i), EDGE, g)

        nothing = lambda: None
        end = SLOTS // 2 - 1
        first(0)
        middle(0, nothing, lambda: first(1))

        @pl.loop(1, end)
        def _(i):
            middle(i, lambda: last(i - 1), lambda: first(i + 1))
        middle(end, lambda: last(end - 1), nothing)
        last(end)

    def backward(first, g):
        @pl.loop(0, SLOTS // 2)
        def _(i):
            backward_rows((2 * i, 2 * i + 1), first, g)

    for side in (0, 1):
        arrived(("col", side), 2, col_s.at[1 - side], col_in.at[side])

        @pl.when(has["col", side])
        def _(side=side):
            for k, strip in enumerate(unpack(col_in.at[side], 0, QUARTER)):
                place_columns(side, MARGIN + k * QUARTER, strip)

    forward(INNER)

    for side in (0, 1):
        first = 0 if side == 0 else TILE - MARGIN
        arrived(("row", side), 0, ob.at[:, pl.ds(0, MARGIN), pl.ds(0, SIDE)], row_in.at[side])
        arrived(("row", side), 7, tail_s.at[1 - side], tail_in.at[side])

        @pl.when(has["row", side])
        def _(side=side, first=first):
            lane = lane_iota(24)
            for h in (0, 1):
                for comp in (0, 1):
                    shift = (HALF - 32 * (2 * h + comp)) % HALF
                    tail = tail_in[side] if shift == 0 else pltpu.roll(tail_in[side], shift, 1)
                    rows = pl.ds(24 * h, 24)
                    place(comp, pl.ds(first + 24 * h, 24),
                          (row_in[side, comp, rows, blk(0)], row_in[side, comp, rows, blk(1)],
                           jnp.where(lane < 32, tail, 0.0)))

        @pl.when(jnp.logical_not(has["row", side]))
        def _(first=first):
            for comp in (0, 1):
                cur[comp, pl.ds(first, MARGIN), :] = jnp.zeros((MARGIN, TILE), F32)
    for a, b in corners:
        arrived((a, b), 1, corner_s.at[1 - b, 1 - a], corner_in.at[b, a])

        @pl.when(peer((a, b))[0])
        def _(a=a, b=b):
            place_columns(b, a * (TILE - MARGIN), corner_in[b, a])

    edge_pass(ga)

    def stage(dst, g, src_row, n_rows):
        for b in range(3):
            for comp in (0, 1):
                dst[b, comp] = g[comp, pl.ds(src_row, n_rows), blk(b)]

    def send_rows(src, dst, kind, blocks):
        for side in (0, 1):
            for b in blocks:
                send(("row", side), kind + (b,), src.at[side, b], dst.at[1 - side, b])

    def add_rows(src, dst, kind, g, first, n_rows, blocks):
        for side in (0, 1):
            for b in blocks:
                arrived(("row", side), kind + (b,), src.at[1 - side, b], dst.at[side, b])

            @pl.when(has["row", side])
            def _(side=side):
                for b in blocks:
                    for comp in (0, 1):
                        g[comp, pl.ds(first[side], n_rows), blk(b)] += dst[side, b, comp]

    for side in (0, 1):
        stage(grow_s.at[side], ga, 0 if side == 0 else TILE - WIDE, WIDE)
    send_rows(grow_s, grow_in, ("g",), (0, 2))
    backward(INNER, ga)

    def gcol_index(part):
        first, second = (WIDE, 2 * WIDE) if part == 0 else (0, TILE - WIDE)
        return [(first + j, second + j, j) for j in range(0, WIDE, MARGIN)]

    def gcol_pack(part):
        n = MARGIN
        lane = lane_iota(n)
        base = part * 288
        for row_a, row_b, j in gcol_index(part):
            for side in (0, 1):
                kept = []
                for row, at in ((row_a, j), (row_b, WIDE + j)):
                    re = ga[0, pl.ds(row, n), blk(0 if side == 0 else 2)]
                    im = ga[1, pl.ds(row, n), blk(0 if side == 0 else 2)]
                    if side == 1:
                        strip = jnp.where(lane < 96, pltpu.roll(re, 96, 1), pltpu.roll(im, 64, 1))
                    else:
                        strip = jnp.where(lane < 96, re, pltpu.roll(im, 96, 1))
                    gcol_s[side, pl.ds(base + at, n), :] = strip
                    kept.append(im)
                shift = (96, 32) if side == 0 else (64, 0)
                low = pltpu.roll(kept[0], shift[0], 1)
                high = pltpu.roll(kept[1], shift[1], 1) if shift[1] else kept[1]
                gcol_s[side, pl.ds(base + 192 + j, n), :] = jnp.where(lane < 64, low, high)

    def gcol_unpack(side, part):
        n = MARGIN
        lane = lane_iota(n)
        base = part * 288
        for row_a, row_b, j in gcol_index(part):
            rest = gcol_in[side, pl.ds(base + 192 + j, n), :]
            for row, at, shift in ((row_a, j, 0), (row_b, WIDE + j, 64)):
                strip = gcol_in[side, pl.ds(base + at, n), :]
                if side == 0:
                    re = jnp.where(lane < 96, strip, 0.0)
                    im = jnp.where(lane < 32, pltpu.roll(strip, 32, 1), pltpu.roll(rest, 32 + shift, 1))
                    im = jnp.where(lane < 96, im, 0.0)
                else:
                    re = jnp.where(lane < 32, 0.0, pltpu.roll(strip, 32, 1))
                    tail = pltpu.roll(rest, 64 + shift, 1) if shift == 0 else rest
                    im = jnp.where(lane < 64, pltpu.roll(strip, 64, 1), tail)
                    im = jnp.where(lane < 32, 0.0, im)
                b = 0 if side == 0 else 2
                ga[0, pl.ds(row, n), blk(b)] += re
                ga[1, pl.ds(row, n), blk(b)] += im

    def gcol_send(part):
        rows = pl.ds(part * 288, 288)
        for side in (0, 1):
            send(("col", side), 3 + part, gcol_s.at[side, rows, :], gcol_in.at[1 - side, rows, :])

    def gcol_add(part):
        rows = pl.ds(part * 288, 288)
        for side in (0, 1):
            arrived(("col", side), 3 + part, gcol_s.at[1 - side, rows, :], gcol_in.at[side, rows, :])

            @pl.when(has["col", side])
            def _(side=side):
                gcol_unpack(side, part)

    def update(rows):
        for at in rows:
            lane = lane_iota(MARGIN)
            ok = True
            if at == 0:
                ok = has["row", 0]
            elif at == TILE - MARGIN:
                ok = has["row", 1]
            keep = (
                jnp.logical_and(ok, jnp.logical_or(lane >= MARGIN, has["col", 0])),
                jnp.logical_and(ok, lane >= 0),
                jnp.logical_and(ok, jnp.logical_or(lane < 80, has["col", 1])),
            )
            for comp in (0, 1):
                for b in range(3):
                    cur[comp, pl.ds(at, MARGIN), blk(b)] += jnp.where(
                        keep[b], STEP * ga[comp, pl.ds(at, MARGIN), blk(b)], 0.0)

    gcol_pack(0)
    gcol_send(0)
    first = (0, TILE - WIDE)
    add_rows(grow_s, grow_in, ("g",), ga, first, WIDE, (0, 2))
    gcol_pack(1)
    gcol_send(1)
    send_rows(grow_s, grow_in, ("g",), (1,))
    gcol_add(0)
    update(range(WIDE, TILE - WIDE, MARGIN))
    forward(INNER)
    gcol_add(1)
    add_rows(grow_s, grow_in, ("g",), ga, first, WIDE, (1,))
    update((0, MARGIN, TILE - WIDE, TILE - MARGIN))

    edge_pass(gb)
    for side in (0, 1):
        stage(frow_s.at[side], gb, 0 if side == 0 else TILE - MARGIN, MARGIN)
    send_rows(frow_s, frow_in, ("f",), (0, 2))
    backward(INNER, gb)

    def fcol_rows(part):
        if part == 0:
            return 0, 48, [WIDE + 48 * k for k in range(4)]
        return 144, 24, [MARGIN, MARGIN + 24, TILE - WIDE, TILE - WIDE + 24]

    def fcol_pack(part):
        base, n, starts = fcol_rows(part)
        for side in (0, 1):
            pack(fcol_s.at[side], base, [
                pair_up(*(gb[comp, pl.ds(row, n), blk(2 * side)] for comp in (0, 1)), 80 * side) for row in starts])

    def fcol_send(part):
        base, n, _ = fcol_rows(part)
        for side in (0, 1):
            rows = pl.ds(base, 3 * n)
            send(("col", side), 5 + part, fcol_s.at[side, rows, :], fcol_in.at[1 - side, rows, :])

    def fcol_add(part):
        base, n, starts = fcol_rows(part)
        rows = pl.ds(base, 3 * n)
        for side in (0, 1):
            arrived(("col", side), 5 + part, fcol_s.at[1 - side, rows, :], fcol_in.at[side, rows, :])

            @pl.when(has["col", side])
            def _(side=side):
                first = MARGIN if side == 0 else 32
                lane = lane_iota(n)
                ok = jnp.logical_and(lane >= first, lane < first + MARGIN)
                for row, strip in zip(starts, unpack(fcol_in.at[side], base, n)):
                    for comp in (0, 1):
                        gb[comp, pl.ds(row, n), blk(2 * side)] += jnp.where(
                            ok, rolled(strip, first - MARGIN * comp), 0.0)

    def write(row):
        lane, rows, to_rows = lane_iota(MARGIN), pl.ds(row, MARGIN), pl.ds(row - MARGIN, MARGIN)
        for comp in (0, 1):
            v = [pltpu.roll(cur[comp, rows, blk(b)] + STEP * gb[comp, rows, blk(b)], 80, 1) for b in range(3)]
            out[comp, to_rows, blk(0)] = jnp.where(lane < 80, v[0], v[1])
            out[comp, to_rows, blk(1)] = jnp.where(lane < 80, v[1], v[2])
            out[comp, to_rows, pl.ds(256, 32)] = v[2][:, :32]

    fcol_pack(0)
    fcol_send(0)
    send_rows(frow_s, frow_in, ("f",), (1,))
    first = (MARGIN, TILE - WIDE)
    add_rows(frow_s, frow_in, ("f",), gb, first, MARGIN, (0, 2))
    fcol_pack(1)
    fcol_send(1)
    fcol_add(0)
    for row in range(WIDE, TILE - WIDE, MARGIN):
        write(row)
    add_rows(frow_s, frow_in, ("f",), gb, first, MARGIN, (1,))
    fcol_add(1)
    for row in first:
        write(row)

    for key, kind, src, dst in started:
        @pl.when(peer(key)[0])
        def _(args=(key, kind, src, dst, True)):
            remote(*args).wait_send()


def shards(object_field, probe, amplitudes, offsets, counts):
    tables = (jnp.asarray(a) for a in half_tables())
    anywhere = pl.BlockSpec(memory_space=pl.ANY)
    scalars = pl.BlockSpec(memory_space=pltpu.SMEM)
    v32 = lambda *shape: pltpu.VMEM(shape, F32)
    v16 = lambda *shape: pltpu.VMEM(shape, BF16)
    return pl.pallas_call(
        kernel,
        out_shape=jax.ShapeDtypeStruct(object_field.shape, F32),
        in_specs=[scalars, scalars] + [anywhere] * 7,
        out_specs=pl.BlockSpec(memory_space=pltpu.VMEM),
        scratch_shapes=[
            v32(2, CORE, CORE), v32(2, SIDE, SIDE), v16(1, 1, SLOTS, SIDE, SIDE),
            v16(SIDE, SIDE), v16(SIDE, SIDE), v16(SIDE, SIDE), v16(SIDE, SIDE),
            v32(SLOTS, 2, SIDE, SIDE), v32(SLOTS, SIDE, SIDE),
            v16(SLOTS, SIDE, 2 * SIDE), v16(2, SIDE, 2 * SIDE), v16(SLOTS, 2 * SIDE, SIDE), v16(2, SIDE, SIDE),
            v32(2, TILE, TILE), v32(2, TILE, TILE), v32(2, TILE, TILE),
            v32(2, 2, MARGIN, SIDE), v32(2, MARGIN // 2, HALF), v32(2, MARGIN // 2, HALF), v32(2, 3 * QUARTER, HALF), v32(2, 3 * QUARTER, HALF),
            v32(2, 2, MARGIN, HALF), v32(2, 2, MARGIN, HALF),
            v32(2, 3, 2, WIDE, HALF), v32(2, 3, 2, WIDE, HALF),
            v32(2, 576, HALF), v32(2, 576, HALF),
            v32(2, 3, 2, MARGIN, HALF), v32(2, 3, 2, MARGIN, HALF),
            v32(2, 216, HALF), v32(2, 216, HALF),
            pltpu.SemaphoreType.DMA((7,)),
            pltpu.SemaphoreType.DMA((30,)),
            pltpu.SemaphoreType.DMA((30,)),
        ],
        compiler_params=pltpu.CompilerParams(
            collective_id=0, has_side_effects=True, vmem_limit_bytes=60 * 1024 * 1024),
        name="ptycho",
    )(jnp.swapaxes(offsets, 2, 3), counts, object_field, probe, amplitudes, *tables)


def solution(mesh):
    return jax.shard_map(
        shards,
        mesh=mesh,
        in_specs=(
            P(None, "row", "col"),
            P(),
            P("row", "col", None, None, None),
            P("row", "col", None, None),
            P("row", "col"),
        ),
        out_specs=P(None, "row", "col"),
        check_vma=False,
    )
```
